128 devices in a mesh: elem: 32 (over y, x, core), face: 4 (over z).
Axes of the slice: x: 4, y: 4, z: 4, core: 2. Of those that a mesh axis runs over, the one named last changes fastest.
Arguments:
- state: float32 [10, 72, 65536], P(None, None, ('elem', 'face')), may hold values from -6 to 6
- metric: float32 [16, 4096], P(None, ('elem', 'face')), may hold values from 0.5 to 2
- neighbours: int32 [4, 4096], P(None, ('elem', 'face')), may hold values from 0 to 4095, as said below
- cost_class: int32 [16, 4096], P(None, ('elem', 'face')), may hold values from 1 to 4
- batch_slot: int32 [16, 4096], replicated, may hold values from 0 to 65535, as said below
- level_mix: float32 [10, 72, 72], replicated, may hold values from -0.75 to 0.75
- field_coupling_matrix: float32 [10, 10], replicated, may hold values from -2 to 2
Outputs:
- state_out: float32 [10, 72, 65536], P(None, None, ('elem', 'face'))
- physics_state: float32 [10, 72, 65536], P(None, None, ('elem', 'face'))
The draws below stay inside these ranges and needn't reach their ends.
Inputs may be any that keep to these rules, and one draw needn't show every extreme that they name: Blocks are the element ranges [b * 32, (b + 1) * 32), in the order of the devices. The elements form a closed grid of rows of 8 elements, 4 rows a block; neighbours[0], [1], [2], [3] name the elements east, west, north and south, which are mutual (the west neighbour of the east one is the element itself, likewise north and south, and east of north is north of east). East and west neighbours lie in the element's own block; a north neighbour lies in the same block or in the next one, a south neighbour in the same block or the previous one, cyclically over the blocks; in each block exactly 8 elements have their north neighbour in the next block and 8 their south neighbour in the previous one. `batch_slot`: A permutation of the columns; batch c holds the places [c * 512, (c + 1) * 512). Every batch holds exactly 4 columns of every block, and within a batch cost_class never rises from one place to the next.
All inputs are finite; a program needn't handle non-finite values.
Results may differ from the reference program's by a relative error of at most 0.0001.
Values sent between devices are 32-bit elements; how exact they have to be, the bound alone decides.
No kernel may reach another device: no remote copies, remote signals or barrier semaphores. Data moves between devices by JAX's collectives and lax.ppermute only.
A program may use at most 128 MiB of HBM per device.

```python
import math
import jax
import jax.numpy as jnp
import numpy as np
from jax import lax

F = 10
L = 72
NP2 = 16
ROWS_DEV = 4
SUBSTEPS = 3
SWEEPS = 4
E_DEV = 32
EW = 8
NELEM = 4096
NCOL = 65536


def invert_ids(permutation):
    extent = permutation.shape[0]
    return jnp.zeros((extent,), jnp.int32).at[permutation].set(jnp.arange(extent, dtype=jnp.int32))


def cost_classes_per_block(key):
    element_blocks = NELEM // E_DEV
    base = jax.random.fold_in(key, 23)
    storm_level = jax.random.randint(jax.random.fold_in(base, 1), (element_blocks,), 0, 4)
    quiet = jax.random.randint(jax.random.fold_in(base, 2), (element_blocks,), 0, 3)
    storm_level = jnp.where(quiet == 0, storm_level, 0)
    chosen = jax.random.randint(jax.random.fold_in(base, 3), (), 0, element_blocks)
    storm_level = jnp.where(jnp.arange(element_blocks) == chosen, 3, storm_level)
    raw_level = jax.random.randint(jax.random.fold_in(base, 4), (NP2, element_blocks, E_DEV), 0, 4)
    raw_level = raw_level.at[0, chosen, 0].set(3)
    return (1 + jnp.minimum(raw_level, storm_level[None, :, None])).astype(jnp.int32)


def draw_neighbours(key, part):
    element_blocks = NELEM // E_DEV
    block_keys = jax.random.split(jax.random.fold_in(key, 11), element_blocks)
    local_order = jax.vmap(lambda inner: jax.random.permutation(inner, E_DEV))(block_keys).astype(jnp.int32)
    slot_ids = local_order + (jnp.arange(element_blocks, dtype=jnp.int32) * E_DEV)[:, None]
    element_grid = slot_ids.reshape(element_blocks * ROWS_DEV, EW)
    east_ids = jnp.roll(element_grid, -1, axis=1)
    west_ids = jnp.roll(element_grid, 1, axis=1)
    north_ids = jnp.roll(element_grid, -1, axis=0)
    south_ids = jnp.roll(element_grid, 1, axis=0)
    neighbour_table = jnp.stack([east_ids, west_ids, north_ids, south_ids]).reshape(4, NELEM)
    flat_ids = element_grid.reshape(NELEM)
    return jnp.zeros((4, NELEM), jnp.int32).at[:, flat_ids].set(neighbour_table)


def draw_cost_class(key, part):
    return cost_classes_per_block(key).reshape(NP2, NELEM)


def draw_batch_slot(key, part):
    element_blocks = NELEM // E_DEV
    width = NP2 * E_DEV
    classes = cost_classes_per_block(key).transpose(1, 0, 2).reshape(element_blocks, width)
    base = jax.random.fold_in(key, 37)
    tie_keys = jax.random.split(jax.random.fold_in(base, 1), element_blocks)
    tie_break = jax.vmap(lambda inner: jax.random.permutation(inner, width))(tie_keys).astype(jnp.int32)
    score = (4 - classes) * width + tie_break
    sorted_order = jnp.argsort(score, axis=1)
    block_rank = jax.vmap(invert_ids)(sorted_order)
    rotation = jax.random.randint(jax.random.fold_in(base, 2), (element_blocks, 1), 0, element_blocks)
    destination = (block_rank + rotation) % element_blocks
    spread = jax.random.permutation(jax.random.fold_in(base, 3), element_blocks * width).astype(jnp.int32).reshape(element_blocks, width)
    global_key = (destination * 4 + (4 - classes)) * (element_blocks * width) + spread
    global_order = jnp.argsort(global_key.reshape(element_blocks * width))
    position = invert_ids(global_order)
    return position.reshape(element_blocks, NP2, E_DEV).transpose(1, 0, 2).reshape(NP2, NELEM)


def level_of(key, shape, pieces, low, top_value):
    loudness = 1.0
    for dim, blocks in pieces:
        steps = jax.random.uniform(jax.random.fold_in(jax.random.fold_in(key, 6), dim), (blocks,), jnp.float32, low / len(pieces), top_value / len(pieces))
        loudness = loudness * jnp.repeat(jnp.exp(steps), shape[dim] // blocks).reshape((-1,) + (1,) * (len(shape) - 1 - dim))
    return loudness


def normal_values(own_key, shape, deviation, limit, cuts=(), kind=jnp.bfloat16):
    loudness = level_of(own_key, shape, cuts, -0.22, 0.18) if cuts else 1.0
    entries = jax.random.normal(own_key, shape, jnp.float32) * deviation * loudness
    return jnp.minimum(jnp.maximum(entries, -limit), limit).astype(kind)


def setup_inputs(seed: int = 0) -> dict:
    keys = jax.random.split(jax.random.key(seed), 8)
    return {
        "state": normal_values(keys[0], (F, L, NCOL), 1.0, 6.0, ((2, 128),), jnp.float32),
        "metric": jnp.clip(jnp.exp(math.log(2.0) - 1.3862944 * jax.random.uniform(keys[1], (NP2, NELEM), jnp.float32) ** level_of(keys[1], (NP2, NELEM), ((1, 128),), -0.2, 0.2)), 0.5, 2.0),
        "neighbours": draw_neighbours(jax.random.fold_in(keys[7], 71), 0),
        "cost_class": draw_cost_class(jax.random.fold_in(keys[7], 71), 0),
        "batch_slot": draw_batch_slot(jax.random.fold_in(keys[7], 71), 0),
        "level_mix": normal_values(keys[5], (F, L, L), L ** -0.5, 0.75, (), jnp.float32),
        "field_coupling_matrix": normal_values(keys[6], (F, F), F ** -0.5, 2.0, (), jnp.float32),
    }


PHYSICS_RATE = 0.1
TIME_STEP = 0.02

def gll_matrices():
    gll_nodes = np.array([-1.0, -1.0 / np.sqrt(5.0), 1.0 / np.sqrt(5.0), 1.0])
    derivative = np.zeros((4, 4))
    for target in range(4):
        for source in range(4):
            if target == source:
                derivative[target, source] = sum((1.0 / (gll_nodes[source] - gll_nodes[middle]) for middle in range(4) if middle != source))
            else:
                numerator = np.prod([gll_nodes[target] - gll_nodes[middle] for middle in range(4) if middle != source and middle != target])
                denominator = np.prod([gll_nodes[source] - gll_nodes[middle] for middle in range(4) if middle != source])
                derivative[target, source] = numerator / denominator
    across = np.kron(np.eye(4), derivative).astype(np.float32)
    upward = np.kron(derivative, np.eye(4)).astype(np.float32)
    return (jnp.asarray(across), jnp.asarray(upward))

def advect(current, across, upward):
    along_x = jnp.einsum('pq,...qe->...pe', across, current, precision=lax.Precision.HIGHEST)
    along_y = jnp.einsum('pq,...qe->...pe', upward, current, precision=lax.Precision.HIGHEST)
    return -(current[0:1] * along_x + current[1:2] * along_y)

def combine(values, neighbours):
    leading = values.shape[:-2]
    members = values.shape[-1]
    layout = values.reshape(leading + (4, 4, members))
    west_edge = layout[..., :, 0, :]
    east_edge = layout[..., :, 3, :]
    new_east = east_edge + jnp.take(west_edge, neighbours[0], axis=-1)
    new_west = west_edge + jnp.take(east_edge, neighbours[1], axis=-1)
    stepped = jnp.stack([new_west, layout[..., :, 1, :], layout[..., :, 2, :], new_east], axis=-2)
    south_row = stepped[..., 0, :, :]
    north_row = stepped[..., 3, :, :]
    north_side = jnp.take(south_row, neighbours[2], axis=-1)
    south_side = jnp.take(north_row, neighbours[3], axis=-1)
    physics_output = jnp.stack([south_row + south_side, stepped[..., 1, :, :], stepped[..., 2, :, :], north_row + north_side], axis=-3)
    return physics_output.reshape(values.shape)

def relax(segment, active, level_mix, field_coupling_matrix):
    level_blended = jnp.einsum('flm,fmc->flc', level_mix, segment, precision=lax.Precision.HIGHEST)
    field_coupled = jnp.einsum('mx,xaq->maq', field_coupling_matrix, level_blended, precision=lax.Precision.HIGHEST)
    return jnp.where(active[None, None, :], segment + PHYSICS_RATE * jnp.tanh(field_coupled), segment)

def reference(state, metric, neighbours, cost_class, batch_slot, level_mix, field_coupling_matrix):
    fields, levels, total = state.shape
    points = metric.shape[0]
    members = metric.shape[1]
    grid_state = jnp.transpose(state.reshape(fields, levels, members, points), (0, 1, 3, 2))
    columns = grid_state.reshape(fields, levels, total)
    weighted = cost_class.reshape(total) * SWEEPS

    def physics_pass(threshold, advanced):
        return relax(advanced, weighted > threshold, level_mix, field_coupling_matrix)
    advanced = lax.fori_loop(0, 4 * SWEEPS, physics_pass, columns)
    physics_state = jnp.zeros_like(advanced).at[:, :, batch_slot.reshape(total)].set(advanced)
    physics_tendency = (advanced - columns).reshape(grid_state.shape)
    across, upward = gll_matrices()
    mass_total = combine(metric, neighbours)

    def per_level(bundle):
        current, change = bundle
        for advection_substep in range(SUBSTEPS):
            rate = advect(current, across, upward)
            updated = current + TIME_STEP * rate + change / SUBSTEPS
            current = combine(metric * updated, neighbours) / mass_total
        return current
    layered = lax.map(per_level, (jnp.moveaxis(grid_state, 1, 0), jnp.moveaxis(physics_tendency, 1, 0)))
    final = jnp.moveaxis(layered, 0, 1)
    state_out = jnp.transpose(final, (0, 1, 3, 2)).reshape(fields, levels, total)
    return (state_out, physics_state)
```

```python
from functools import partial

import jax
import jax.numpy as jnp
import numpy as np
from jax import lax
from jax.experimental import pallas as pl
from jax.experimental.pallas import tpu as pltpu
from jax.sharding import PartitionSpec as P

AXES = ("elem", "face")
F32 = jnp.float32
BF16 = jnp.bfloat16
HIGHEST = lax.Precision.HIGHEST
FIELDS, LEVELS, SUBSTEPS = 10, 72, 3
ROWS, COLS, MEMBERS, WIDE = 720, 512, 32, 768
TALL = ROWS + 8
PHYSICS_RATE, TIME_STEP = 0.1, 0.02
VM = pl.BlockSpec(memory_space=pltpu.VMEM)
SM = pl.BlockSpec(memory_space=pltpu.SMEM)
PARAMS = pltpu.CompilerParams(vmem_limit_bytes=60 << 20)


def gll_matrix():
    nodes = np.array([-1.0, -1.0 / np.sqrt(5.0), 1.0 / np.sqrt(5.0), 1.0])
    derivative = np.zeros((4, 4))
    for i in range(4):
        for j in range(4):
            others = [k for k in range(4) if k != j]
            if i == j:
                derivative[i, j] = sum(1.0 / (nodes[j] - nodes[k]) for k in others)
            else:
                top = np.prod([nodes[i] - nodes[k] for k in others if k != i])
                derivative[i, j] = top / np.prod([nodes[j] - nodes[k] for k in others])
    return derivative


def derivative_blocks():
    d = gll_matrix()
    across = np.kron(np.eye(4), d).astype(np.float32).T
    upward = np.kron(d, np.eye(4)).astype(np.float32).T
    return np.kron(np.eye(16), across).astype(np.float32), np.kron(np.eye(16), upward).astype(np.float32)

def split2(v):
    hi = v.astype(BF16)
    return hi, (v - hi.astype(F32)).astype(BF16)


def dot(a, b):
    return jnp.dot(a, b, preferred_element_type=F32)


def dot_nt(a, b):
    return lax.dot_general(a, b, (((1,), (1,)), ((), ())), preferred_element_type=F32)


def iota(shape, dim):
    return lax.broadcasted_iota(jnp.int32, shape, dim)


def expand_points(table):
    spread = jnp.where(iota((32, COLS), 1) // 16 == iota((32, COLS), 0), 1.0, 0.0)
    wide = jnp.dot(table, spread, precision=HIGHEST, preferred_element_type=F32)
    wide = jnp.where(iota((16, COLS), 1) % 16 == iota((16, COLS), 0), wide, 0.0)
    return jnp.sum(wide, axis=0, keepdims=True)


def as_column(row):
    return jnp.transpose(jnp.broadcast_to(row, (8, COLS)))[:, 0:1]


def rank_row(key_row):
    key_col = as_column(key_row)
    return jnp.sum(jnp.where(key_col < key_row, 1.0, 0.0), axis=0, keepdims=True)


def physics_kernel(fcm_ref, state_ref, class_ref, slot_ref, mix_ref, send_ref, tend_ref,
                   k32, kh, kl, x0, yy, tt, rr, qq, pp):
    rep = jnp.where(
        (iota((72, WIDE), 1) % 72 == iota((72, WIDE), 0)) & (iota((72, WIDE), 1) < ROWS), 1.0, 0.0)
    lane = iota((1, WIDE), 1)
    for f in range(10):
        crow = jnp.zeros((1, WIDE), F32)
        for g in range(10):
            crow = jnp.where((lane >= 72 * g) & (lane < 72 * g + 72), fcm_ref[g, f], crow)
        tiled = jnp.dot(jnp.transpose(mix_ref[f]), rep, precision=HIGHEST, preferred_element_type=F32)
        k32[72 * f:72 * f + 72, :] = tiled * crow
    k32[ROWS:WIDE, :] = jnp.zeros((WIDE - ROWS, WIDE), F32)
    hi, lo = split2(k32[...])
    kh[...] = hi
    kl[...] = lo
    cls = expand_points(class_ref[...].astype(F32))
    slot = expand_points(slot_ref[...].astype(F32))
    col = iota((1, COLS), 1).astype(F32)
    crank = rank_row((4.0 - cls) * COLS + col)
    srank = rank_row(slot)
    place = slot - jnp.floor(slot * (1.0 / COLS)) * COLS
    perm = jnp.where(iota((COLS, COLS), 0).astype(F32) == crank, 1.0, 0.0).astype(BF16)
    pp[...] = perm
    sh, sl = split2(state_ref[...])
    x0[:, 0:ROWS] = dot_nt(perm, sh) + dot_nt(perm, sl)
    extra = jnp.where(iota((128, COLS), 0) == 0, place, jnp.where(iota((128, COLS), 0) == 1, srank, 0.0))
    eh, el = split2(extra)
    tail = dot_nt(perm, eh) + dot_nt(perm, el)
    x0[:, ROWS:WIDE] = tail[:, 0:WIDE - ROWS]
    eh8, el8 = split2(jnp.broadcast_to(srank, (16, COLS)))
    srank_sorted = (dot_nt(eh8, perm) + dot_nt(el8, perm))[0:1, :]
    n1 = jnp.sum(jnp.where(cls > 1.5, 1, 0))
    n2 = jnp.sum(jnp.where(cls > 2.5, 1, 0))
    n3 = jnp.sum(jnp.where(cls > 3.5, 1, 0))
    xh, xl = split2(x0[...])
    yy[...] = dot(xh, kh[...]) + dot(xl, kh[...]) + dot(xh, kl[...])
    tt[...] = jnp.zeros((COLS, WIDE), F32)
    rr[...] = jnp.zeros((COLS, WIDE), F32)

    def rows_step(rows, live):
        for b in range(0, rows, 64):
            at = pl.ds(b, 64)
            t = jnp.tanh(yy[at, :])
            active = iota((64, WIDE), 0) + b < live
            tt[at, :] += jnp.where(active, t, 0.0)
            s = t + rr[at, :]
            q = s.astype(BF16)
            rr[at, :] = s - q.astype(F32)
            qq[at, :] = q
        q = qq[0:rows, :]
        yy[0:rows, :] += 0.1 * (dot(q, kh[...]) + dot(q, kl[...]))

    def sweep(k, _):
        live = jnp.where(k < 4, COLS, jnp.where(k < 8, n1, jnp.where(k < 12, n2, n3)))
        sizes = [64 * (i + 1) for i in range(8)]
        which = (live + 63) // 64
        for i, rows in enumerate(sizes):
            @pl.when(which == i + 1)
            def _():
                rows_step(rows, live)
        return 0

    lax.fori_loop(0, 16, sweep, 0)
    q_send = jnp.where(iota((COLS, COLS), 0).astype(F32) == srank_sorted, 1.0, 0.0).astype(BF16)
    fh, fl = split2(x0[...] + 0.1 * tt[...])
    out = dot(q_send, fh) + dot(q_send, fl)
    send_ref[...] = out.reshape(COLS // 4, 4, WIDE)
    th, tl = split2(jnp.transpose(tt[...])[0:ROWS, :] * (0.1 / 3.0))
    tend_ref[...] = dot(th, perm) + dot(tl, perm)


def physics_call(state2, cost_class, slots, level_mix, fcm):
    return call(
        physics_kernel, "physics", [((COLS // 4, 4, WIDE), F32), ((ROWS, COLS), F32)], [SM, VM, VM, VM, VM],
        [((WIDE, WIDE), F32), ((WIDE, WIDE), BF16), ((WIDE, WIDE), BF16)] + [((COLS, WIDE), F32)] * 4
        + [((COLS, WIDE), BF16), ((COLS, COLS), BF16)],
    )(fcm, state2, cost_class, slots, level_mix)


def element_tables(neighbours_ref, base_ref):
    local = neighbours_ref[...] - base_ref[0]
    outside = (local < 0) | (local >= MEMBERS)
    wide = jnp.concatenate([local.astype(F32), jnp.where(outside, 1.0, 0.0)], axis=0)
    spread = jnp.where(iota((MEMBERS, COLS), 1) // 16 == iota((MEMBERS, COLS), 0), 1.0, 0.0)
    by_column = jnp.dot(wide, spread, precision=HIGHEST, preferred_element_type=F32)
    return wide, by_column, spread


def east_west(by_column):
    col = iota((1, COLS), 1)
    ix, line = col % 4, (col % 16) // 4 * 4
    source = jnp.where(ix == 3, 16.0 * by_column[0:1] + line.astype(F32),
                       jnp.where(ix == 0, 16.0 * by_column[1:2] + (line + 3).astype(F32), -1.0))
    row = iota((COLS, COLS), 0)
    hit = (row.astype(F32) == source) | (row == iota((COLS, COLS), 1))
    return jnp.where(hit, 1.0, 0.0).astype(BF16)


def north_south(by_column):
    col = iota((1, COLS), 1)
    ix, iy = (col % 4).astype(F32), (col % 16) // 4
    north = jnp.where(by_column[6:7] > 0.5, -1.0, 16.0 * by_column[2:3] + ix)
    south = jnp.where(by_column[7:8] > 0.5, -1.0, 16.0 * by_column[3:4] + 12.0 + ix)
    source = jnp.where(iy == 3, north, jnp.where(iy == 0, south, -1.0))
    row = iota((COLS, COLS), 0)
    hit = (row.astype(F32) == source) | (row == iota((COLS, COLS), 1))
    return jnp.where(hit, 1.0, 0.0).astype(BF16)


def rank_among(key, member, spread):
    key8 = jnp.broadcast_to(jnp.where(member > 0.5, key, 1e9), (8, MEMBERS))
    key_col = jnp.transpose(key8)[:, 0:1]
    rank = jnp.sum(jnp.where(key_col < key, 1.0, 0.0), axis=0, keepdims=True)
    return jnp.dot(jnp.broadcast_to(rank, (8, MEMBERS)), spread, precision=HIGHEST,
                   preferred_element_type=F32)[0:1]


def halo_targets(wide, by_column, spread):
    col = iota((1, COLS), 1)
    ix, iy = (col % 4).astype(F32), (col % 16) // 4
    own = iota((1, MEMBERS), 1).astype(F32)
    up, down = by_column[6:7] > 0.5, by_column[7:8] > 0.5
    to_north = jnp.where((iy == 3) & up, 8.0 * ix + rank_among(own, wide[6:7], spread), -1.0)
    to_south = jnp.where((iy == 0) & down, 8.0 * ix + rank_among(own, wide[7:8], spread), -1.0)
    from_south = jnp.where((iy == 0) & down, 8.0 * ix + rank_among(wide[3:4], wide[7:8], spread), -1.0)
    from_north = jnp.where((iy == 3) & up, 8.0 * ix + rank_among(wide[2:3], wide[6:7], spread), -1.0)
    return to_north, to_south, from_south, from_north


def two_selections(first, second):
    row = iota((2 * MEMBERS, COLS), 0).astype(F32)
    hit = (row == first) | ((row - MEMBERS == second) & (second > -0.5))
    return jnp.where(hit, 1.0, 0.0).astype(BF16)


def tables_kernel(base_ref, neighbours_ref, metric_ref, whole_ref, out_ref, in_ref, mrow_ref):
    wide, by_column, spread = element_tables(neighbours_ref, base_ref)
    along = east_west(by_column)
    whole_ref[...] = dot(along, north_south(by_column)).astype(BF16)
    to_north, to_south, from_south, from_north = halo_targets(wide, by_column, spread)
    out_ref[...] = dot_nt(two_selections(to_north, to_south), along).astype(BF16)
    in_ref[...] = two_selections(from_south, from_north)
    mrow_ref[...] = jnp.broadcast_to(expand_points(metric_ref[...]), (8, COLS))


def move(read, tend_ref, mrow_ref, dx_ref, dy_ref, out_ref, dxs, dys, m_ref, north_ref, south_ref):
    vh, vl = split2(read(0, ROWS))
    for half in (0, 256):
        at = slice(half, half + 256)
        for d_ref, acc in ((dx_ref, dxs), (dy_ref, dys)):
            dh, dl = split2(d_ref[...])
            acc[:, at] = dot(vh[:, at], dh) + dot(vl[:, at], dh) + dot(vh[:, at], dl)
    metric = mrow_ref[0:1, :]
    u, v = read(0, LEVELS), read(LEVELS, LEVELS)
    for f in range(FIELDS):
        at = pl.ds(LEVELS * f, LEVELS)
        rate = u * dxs[at, :] + v * dys[at, :]
        m_ref[at, :] = metric * ((read(LEVELS * f, LEVELS) - TIME_STEP * rate) + tend_ref[at, :])
    m_ref[ROWS:TALL, :] = mrow_ref[...]
    mh, ml = split2(m_ref[...])
    halo = dot_nt(out_ref[...], mh) + dot_nt(out_ref[...], ml)
    north_ref[:, 0:TALL] = halo[0:MEMBERS]
    south_ref[:, 0:TALL] = halo[MEMBERS:]
    north_ref[:, TALL:WIDE] = jnp.zeros((MEMBERS, WIDE - TALL), F32)
    south_ref[:, TALL:WIDE] = jnp.zeros((MEMBERS, WIDE - TALL), F32)


def first_kernel(state_ref, tend_ref, mrow_ref, dx_ref, dy_ref, out_ref, m_ref, north_ref, south_ref, dxs, dys):
    move(lambda at, n: state_ref[pl.ds(at, n), :], tend_ref, mrow_ref, dx_ref, dy_ref, out_ref,
         dxs, dys, m_ref, north_ref, south_ref)


def sum_kernel(m_ref, whole_ref, l_ref):
    mh, ml = split2(m_ref[...])
    l_ref[...] = dot(mh, whole_ref[...]) + dot(ml, whole_ref[...])


def finish(l_ref, prev_ref, next_ref, in_ref, c_ref):
    halo = jnp.concatenate([prev_ref[...], next_ref[...]], axis=0)
    hh, hl = split2(jnp.transpose(halo)[0:TALL, :])
    total = l_ref[...] + dot(hh, in_ref[...]) + dot(hl, in_ref[...])
    c_ref[...] = total[0:ROWS, :] / total[ROWS:ROWS + 1, :]


def next_kernel(l_ref, prev_ref, next_ref, in_ref, tend_ref, mrow_ref, dx_ref, dy_ref, out_ref,
                m_ref, north_ref, south_ref, cur, dxs, dys):
    finish(l_ref, prev_ref, next_ref, in_ref, cur)
    move(lambda at, n: cur[pl.ds(at, n), :], tend_ref, mrow_ref, dx_ref, dy_ref, out_ref,
         dxs, dys, m_ref, north_ref, south_ref)


def place_kernel(arrived_ref, out_ref):
    rows = arrived_ref[...].reshape(COLS, WIDE)
    turned = jnp.transpose(rows)
    place_col = rows[:, ROWS:ROWS + 1]
    pick = jnp.where(iota((COLS, COLS), 1).astype(F32) == place_col, 1.0, 0.0).astype(BF16)
    hi, lo = split2(turned[0:ROWS, :])
    out_ref[...] = dot(hi, pick) + dot(lo, pick)


def call(kernel, name, out, specs, scratch=()):
    shapes = tuple(jax.ShapeDtypeStruct(s, t) for s, t in out)
    return pl.pallas_call(
        kernel, out_shape=shapes, in_specs=specs, out_specs=(VM,) * len(out),
        scratch_shapes=[pltpu.VMEM(s, t) for s, t in scratch], compiler_params=PARAMS, name=name)


def shifted(array, by):
    length = lax.axis_size(AXES)
    return lax.ppermute(array, AXES, [(i, (i + by) % length) for i in range(length)])


def per_device(state, metric, neighbours, cost_class, batch_slot, level_mix, field_coupling_matrix):
    myself = lax.axis_index(AXES)
    state2 = state.reshape(ROWS, COLS)
    slots = lax.dynamic_slice_in_dim(batch_slot, myself * MEMBERS, MEMBERS, axis=1)
    base = (myself * MEMBERS).astype(jnp.int32).reshape(1)
    dx, dy = (jnp.asarray(a) for a in derivative_blocks())
    send, tend = physics_call(state2, cost_class, slots, level_mix, field_coupling_matrix)
    whole, out_rows, in_rows, mrow = call(
        tables_kernel, "tables",
        [((COLS, COLS), BF16), ((2 * MEMBERS, COLS), BF16), ((2 * MEMBERS, COLS), BF16), ((8, COLS), F32)],
        [SM, VM, VM])(base, neighbours, metric)
    moved_out = [((TALL, COLS), F32), ((MEMBERS, WIDE), F32), ((MEMBERS, WIDE), F32)]
    work = [((ROWS, COLS), F32)] * 2
    arrived = lax.all_to_all(send, AXES, split_axis=0, concat_axis=0, tiled=True)
    m, north, south = call(first_kernel, "first", moved_out, [VM] * 6, work)(
        state2, tend, mrow, dx, dy, out_rows)
    for substep in range(SUBSTEPS):
        from_prev, from_next = shifted(north, 1), shifted(south, -1)
        (total,) = call(sum_kernel, "sum", [((TALL, COLS), F32)], [VM, VM])(m, whole)
        if substep < SUBSTEPS - 1:
            m, north, south = call(next_kernel, "next", moved_out, [VM] * 9, work + work[:1])(
                total, from_prev, from_next, in_rows, tend, mrow, dx, dy, out_rows)
    (state_out,) = call(finish, "finish", [((ROWS, COLS), F32)], [VM] * 4)(total, from_prev, from_next, in_rows)
    (physics_state,) = call(place_kernel, "place", [((ROWS, COLS), F32)], [VM])(arrived)
    return state_out.reshape(state.shape), physics_state.reshape(state.shape)


def solution(mesh):
    split = P(None, AXES)
    whole = P(None, None, AXES)
    return jax.shard_map(
        per_device, mesh=mesh, in_specs=(whole, split, split, split, P(), P(), P()),
        out_specs=(whole, whole), check_vma=False)
```

```python
import jax
import jax.numpy as jnp
import numpy as np
from jax import lax
from jax.experimental import pallas as pl
from jax.experimental.pallas import tpu as pltpu
from jax.sharding import PartitionSpec as P


AXES = ("elem", "face")
F32 = jnp.float32
BF16 = jnp.bfloat16
HIGHEST = lax.Precision.HIGHEST
FIELDS, LEVELS, SUBSTEPS = 10, 72, 3
ROWS, COLS, MEMBERS, WIDE = 720, 512, 32, 768
TALL = ROWS + 8
PHYSICS_RATE, TIME_STEP = 0.1, 0.02
VM = pl.BlockSpec(memory_space=pltpu.VMEM)
HB = pl.BlockSpec(memory_space=pltpu.HBM)
SM = pl.BlockSpec(memory_space=pltpu.SMEM)
PARAMS = pltpu.CompilerParams(vmem_limit_bytes=30 << 20)


def gll_matrix():
    nodes = np.array([-1.0, -1.0 / np.sqrt(5.0), 1.0 / np.sqrt(5.0), 1.0])
    derivative = np.zeros((4, 4))
    for i in range(4):
        for j in range(4):
            others = [k for k in range(4) if k != j]
            if i == j:
                derivative[i, j] = sum(1.0 / (nodes[j] - nodes[k]) for k in others)
            else:
                top = np.prod([nodes[i] - nodes[k] for k in others if k != i])
                derivative[i, j] = top / np.prod([nodes[j] - nodes[k] for k in others])
    return derivative


def derivative_blocks():
    d = gll_matrix()
    across = np.kron(np.eye(4), d).astype(np.float32).T
    upward = np.kron(d, np.eye(4)).astype(np.float32).T
    return np.kron(np.eye(16), across).astype(np.float32), np.kron(np.eye(16), upward).astype(np.float32)


def split2(v):
    hi = v.astype(BF16)
    return hi, (v - hi.astype(F32)).astype(BF16)


def dot(a, b):
    return jnp.dot(a, b, preferred_element_type=F32)


def dot_nt(a, b):
    return lax.dot_general(a, b, (((1,), (1,)), ((), ())), preferred_element_type=F32)


def iota(shape, dim):
    return lax.broadcasted_iota(jnp.int32, shape, dim)


def expand_points(table):
    spread = jnp.where(iota((32, COLS), 1) // 16 == iota((32, COLS), 0), 1.0, 0.0)
    wide = jnp.dot(table, spread, precision=HIGHEST, preferred_element_type=F32)
    wide = jnp.where(iota((16, COLS), 1) % 16 == iota((16, COLS), 0), wide, 0.0)
    return jnp.sum(wide, axis=0, keepdims=True)


def as_column(row):
    return jnp.transpose(jnp.broadcast_to(row, (8, COLS)))[:, 0:1]


def rank_row(key_row):
    key_col = as_column(key_row)
    return jnp.sum(jnp.where(key_col < key_row, 1.0, 0.0), axis=0, keepdims=True)


def physics_kernel(me_ref, fcm_hbm, state_hbm, class_hbm, slots_hbm, mix_hbm, metric_hbm, nb_hbm, dx_hbm, dy_hbm,
                   send_hbm, tend_ref, m_ref, mine_a_ref, mine_b_ref, out_ref, in_ref, mrow_ref,
                   k32, kk, state_ref, class_ref, slot_ref, mix_ref, x0, yy, tt, rr, qa, qb, send_ref,
                   metric_ref, nb_ref, dx_ref, dy_ref, dxs, dys, fcm_ref, sems):
    me = me_ref[0]
    load_slots = pltpu.make_async_copy(
        slots_hbm.at[:, pl.ds(pl.multiple_of(me // 4 * 128, 128), 128)], slot_ref, sems.at[0])
    load_state = pltpu.make_async_copy(state_hbm, state_ref, sems.at[1])
    load_class = pltpu.make_async_copy(class_hbm, class_ref, sems.at[2])
    load_mix = pltpu.make_async_copy(mix_hbm, mix_ref, sems.at[3])
    load_fcm = pltpu.make_async_copy(fcm_hbm, fcm_ref, sems.at[4])
    load_metric = pltpu.make_async_copy(metric_hbm, metric_ref, sems.at[5])
    load_nb = pltpu.make_async_copy(nb_hbm, nb_ref, sems.at[6])
    load_dx = pltpu.make_async_copy(dx_hbm, dx_ref, sems.at[7])
    load_dy = pltpu.make_async_copy(dy_hbm, dy_ref, sems.at[8])
    load_fcm.start()
    load_mix.start()
    load_slots.start()
    load_class.start()
    load_state.start()
    load_nb.start()
    load_metric.start()
    load_dx.start()
    load_dy.start()
    rep = jnp.where(
        (iota((LEVELS, WIDE), 1) % LEVELS == iota((LEVELS, WIDE), 0)) & (iota((LEVELS, WIDE), 1) < ROWS), 1.0, 0.0
    ).astype(BF16)
    lane = iota((1, WIDE), 1)
    load_fcm.wait()
    load_mix.wait()
    for f in range(FIELDS):
        crow = jnp.zeros((1, WIDE), F32)
        for g in range(FIELDS):
            crow = jnp.where((lane >= LEVELS * g) & (lane < LEVELS * g + LEVELS), PHYSICS_RATE * fcm_ref[g, f], crow)
        mh, ml = split2(jnp.transpose(mix_ref[f]))
        k32[LEVELS * f:LEVELS * f + LEVELS, :] = (dot(mh, rep) + dot(ml, rep)) * crow
    k32[ROWS:WIDE, :] = jnp.zeros((WIDE - ROWS, WIDE), F32)
    hi, lo = split2(k32[...])
    kk[0:WIDE, :] = hi
    kk[WIDE:, :] = lo
    load_slots.wait()
    load_class.wait()
    part = me % 4
    own = slot_ref[:, 0:MEMBERS]
    for j in range(1, 4):
        own = jnp.where(part == j, slot_ref[:, MEMBERS * j:MEMBERS * j + MEMBERS], own)
    cls = expand_points(class_ref[...].astype(F32))
    slot = expand_points(own.astype(F32))
    col = iota((1, COLS), 1).astype(F32)
    crank = rank_row((4.0 - cls) * COLS + col)
    srank = rank_row(slot)
    place = slot - jnp.floor(slot * (1.0 / COLS)) * COLS
    perm = jnp.where(iota((COLS, COLS), 0).astype(F32) == crank, 1.0, 0.0).astype(BF16)
    extra = jnp.where(iota((128, COLS), 0) == 0, place, 0.0)
    eh, el = split2(extra)
    x0[:, ROWS:WIDE] = (dot_nt(perm, eh) + dot_nt(perm, el))[:, 0:WIDE - ROWS]
    rh, rl = split2(jnp.broadcast_to(srank, (16, COLS)))
    srank_sorted = (dot_nt(rh, perm) + dot_nt(rl, perm))[0:1, :]
    n1 = jnp.sum(jnp.where(cls > 1.5, 1, 0))
    n2 = jnp.sum(jnp.where(cls > 2.5, 1, 0))
    n3 = jnp.sum(jnp.where(cls > 3.5, 1, 0))
    load_state.wait()
    sh, sl = split2(state_ref[...])
    x0[:, 0:ROWS] = dot_nt(perm, sh) + dot_nt(perm, sl)
    xh, xl = split2(x0[...])
    xhh = jnp.concatenate([xh, xh], axis=1)
    for n in range(0, WIDE, 256):
        at = slice(n, n + 256)
        y = (dot(xl, kk[0:WIDE, at]) + dot(xhh, kk[:, at])) * (1.0 / PHYSICS_RATE)
        yy[:, at] = y
        t = jnp.tanh(y)
        tt[:, at] = t
        q = t.astype(BF16)
        rr[:, at] = t - q.astype(F32)
        qa[:, at] = q

    def step(rows, live, old, new, low):
        deep = 2 * WIDE if low else WIDE
        n, wd, at, br = 0, WIDE, slice(0, WIDE), 64
        acc = dot(old[0:rows, 0:deep], kk[0:deep, :])
        for b in range(0, rows, br):
            part = acc[b:b + br]
            rb = slice(b, b + br)
            y = yy[rb, at] + part
            yy[rb, at] = y
            t = jnp.tanh(y)
            if b + 64 >= rows:
                tt[rb, at] += jnp.where(iota((br, wd), 0) + b < live, t, 0.0)
            else:
                tt[rb, at] += t
            s = t + rr[rb, at]
            q = s.astype(BF16)
            rr[rb, at] = s - q.astype(F32)
            new[rb, at] = q
            if not low:
                new[rb, WIDE + n:WIDE + n + wd] = (old[rb, at].astype(F32) + q.astype(F32)).astype(BF16)

    def sweep(k, old, new, low):
        live = jnp.where(k < 4, COLS, jnp.where(k < 8, n1, jnp.where(k < 12, n2, jnp.where(k < 16, n3, 0))))
        which = (live + 63) // 64
        for i in range(8):
            @pl.when(which == i + 1)
            def _():
                step(64 * (i + 1), live, old, new, low)

    def two_sweeps(j, _):
        sweep(2 * j + 1, qa, qb, False)
        sweep(2 * j + 2, qb, qa, True)
        return 0

    lax.fori_loop(0, 8, two_sweeps, 0)
    q_send = jnp.where(iota((COLS, COLS), 0).astype(F32) == srank_sorted, 1.0, 0.0).astype(BF16)
    fh, fl = split2(x0[...] + PHYSICS_RATE * tt[...])
    out = dot(q_send, fh) + dot(q_send, fl)
    send_ref[...] = out.reshape(COLS // 4, 4, WIDE)
    store_send = pltpu.make_async_copy(send_ref, send_hbm, sems.at[9])
    store_send.start()
    th, tl = split2(jnp.transpose(tt[...])[0:ROWS, :] * (PHYSICS_RATE / SUBSTEPS))
    tend_ref[...] = dot(th, perm) + dot(tl, perm)
    load_nb.wait()
    load_metric.wait()
    tables(me * MEMBERS, nb_ref, metric_ref, out_ref, in_ref, mrow_ref)
    load_dx.wait()
    load_dy.wait()
    move(lambda at, n: state_ref[pl.ds(at, n), :], tend_ref, mrow_ref, dx_ref, dy_ref, out_ref,
         dxs, dys, m_ref, mine_a_ref, mine_b_ref)
    store_send.wait()


HALO = ((MEMBERS, WIDE), F32)
MOVED = ((TALL, COLS), F32)
GRID = ((ROWS, COLS), F32)


def physics_call(state2, cost_class, batch_slot, level_mix, fcm, me, metric, neighbours, dx, dy):
    work = [((WIDE, WIDE), F32), ((2 * WIDE, WIDE), BF16), GRID, ((16, MEMBERS), jnp.int32),
            ((16, 128), jnp.int32), ((FIELDS, LEVELS, LEVELS), F32)]
    work += [((COLS, WIDE), F32)] * 4 + [((COLS, WIDE), BF16), ((COLS, 2 * WIDE), BF16), ((COLS // 4, 4, WIDE), F32)]
    work += [((16, MEMBERS), F32), ((4, MEMBERS), jnp.int32), ((256, 256), F32), ((256, 256), F32), GRID, GRID]
    out = [((COLS // 4, 4, WIDE), F32), GRID, MOVED, HALO, HALO, ((2 * MEMBERS, COLS), BF16),
           ((2 * MEMBERS, COLS), BF16), ((8, COLS), F32)]
    shapes = tuple((pltpu.HBM if k < 1 else pltpu.VMEM)(s, t) for k, (s, t) in enumerate(out))
    return pl.pallas_call(
        physics_kernel, out_shape=shapes, in_specs=[SM] + [HB] * 9, out_specs=(HB,) + (VM,) * 7,
        scratch_shapes=[pltpu.VMEM(s, t) for s, t in work]
        + [pltpu.SMEM((FIELDS, FIELDS), F32), pltpu.SemaphoreType.DMA((10,))],
        compiler_params=PARAMS, name="physics",
    )(me, *in_hbm(fcm, state2, cost_class, batch_slot, level_mix, metric, neighbours, dx, dy))


def element_tables(neighbours_ref, base):
    local = neighbours_ref[...] - base
    outside = (local < 0) | (local >= MEMBERS)
    wide = jnp.concatenate([local.astype(F32), jnp.where(outside, 1.0, 0.0)], axis=0)
    spread = jnp.where(iota((MEMBERS, COLS), 1) // 16 == iota((MEMBERS, COLS), 0), 1.0, 0.0)
    by_column = jnp.dot(wide, spread, precision=HIGHEST, preferred_element_type=F32)
    return wide, by_column, spread


def east_west(by_column):
    col = iota((1, COLS), 1)
    ix, line = col % 4, (col % 16) // 4 * 4
    source = jnp.where(ix == 3, 16.0 * by_column[0:1] + line.astype(F32),
                       jnp.where(ix == 0, 16.0 * by_column[1:2] + (line + 3).astype(F32), -1.0))
    row = iota((COLS, COLS), 0)
    hit = (row.astype(F32) == source) | (row == iota((COLS, COLS), 1))
    return jnp.where(hit, 1.0, 0.0).astype(BF16)


def north_south(by_column):
    col = iota((1, COLS), 1)
    ix, iy = (col % 4).astype(F32), (col % 16) // 4
    north = jnp.where(by_column[6:7] > 0.5, -1.0, 16.0 * by_column[2:3] + ix)
    south = jnp.where(by_column[7:8] > 0.5, -1.0, 16.0 * by_column[3:4] + 12.0 + ix)
    source = jnp.where(iy == 3, north, jnp.where(iy == 0, south, -1.0))
    row = iota((COLS, COLS), 0)
    hit = (row.astype(F32) == source) | (row == iota((COLS, COLS), 1))
    return jnp.where(hit, 1.0, 0.0).astype(BF16)


def rank_among(key, member, spread):
    key8 = jnp.broadcast_to(jnp.where(member > 0.5, key, 1e9), (8, MEMBERS))
    key_col = jnp.transpose(key8)[:, 0:1]
    rank = jnp.sum(jnp.where(key_col < key, 1.0, 0.0), axis=0, keepdims=True)
    return jnp.dot(jnp.broadcast_to(rank, (8, MEMBERS)), spread, precision=HIGHEST,
                   preferred_element_type=F32)[0:1]


def halo_targets(wide, by_column, spread):
    col = iota((1, COLS), 1)
    ix, iy = (col % 4).astype(F32), (col % 16) // 4
    own = iota((1, MEMBERS), 1).astype(F32)
    up, down = by_column[6:7] > 0.5, by_column[7:8] > 0.5
    to_north = jnp.where((iy == 3) & up, 8.0 * ix + rank_among(own, wide[6:7], spread), -1.0)
    to_south = jnp.where((iy == 0) & down, 8.0 * ix + rank_among(own, wide[7:8], spread), -1.0)
    from_south = jnp.where((iy == 0) & down, 8.0 * ix + rank_among(wide[3:4], wide[7:8], spread), -1.0)
    from_north = jnp.where((iy == 3) & up, 8.0 * ix + rank_among(wide[2:3], wide[6:7], spread), -1.0)
    return to_north, to_south, from_south, from_north


def two_selections(first, second):
    row = iota((2 * MEMBERS, COLS), 0).astype(F32)
    hit = (row == first) | ((row - MEMBERS == second) & (second > -0.5))
    return jnp.where(hit, 1.0, 0.0).astype(BF16)


def whole_kernel(base_ref, neighbours_ref, whole_ref):
    base = base_ref[0]
    _, by_column, _ = element_tables(neighbours_ref, base)
    whole_ref[...] = dot(east_west(by_column), north_south(by_column)).astype(BF16)


def tables(base, neighbours_ref, metric_ref, out_ref, in_ref, mrow_ref):
    wide, by_column, spread = element_tables(neighbours_ref, base)
    to_north, to_south, from_south, from_north = halo_targets(wide, by_column, spread)
    odd = base // MEMBERS % 2 == 1
    sent = two_selections(jnp.where(odd, to_south, to_north), jnp.where(odd, to_north, to_south))
    out_ref[...] = dot_nt(sent, east_west(by_column)).astype(BF16)
    in_ref[...] = two_selections(jnp.where(odd, from_south, from_north), jnp.where(odd, from_north, from_south))
    mrow_ref[...] = jnp.broadcast_to(expand_points(metric_ref[...]), (8, COLS))


def move(read, tend_ref, mrow_ref, dx_ref, dy_ref, out_ref, dxs, dys, m_ref, north_ref, south_ref):
    vh, vl = split2(read(0, ROWS))
    for half in (0, 256):
        at = slice(half, half + 256)
        for d_ref, acc in ((dx_ref, dxs), (dy_ref, dys)):
            dh, dl = split2(d_ref[...])
            acc[:, at] = dot(vh[:, at], dh) + dot(vl[:, at], dh) + dot(vh[:, at], dl)
    metric = mrow_ref[0:1, :]
    u, v = read(0, LEVELS), read(LEVELS, LEVELS)
    for f in range(FIELDS):
        at = pl.ds(LEVELS * f, LEVELS)
        rate = u * dxs[at, :] + v * dys[at, :]
        m_ref[at, :] = metric * ((read(LEVELS * f, LEVELS) - TIME_STEP * rate) + tend_ref[at, :])
    m_ref[ROWS:TALL, :] = mrow_ref[...]
    mh, ml = split2(m_ref[...])
    halo = dot_nt(out_ref[...], mh) + dot_nt(out_ref[...], ml)
    north_ref[:, 0:TALL] = halo[0:MEMBERS]
    south_ref[:, 0:TALL] = halo[MEMBERS:]
    north_ref[:, TALL:WIDE] = jnp.zeros((MEMBERS, WIDE - TALL), F32)
    south_ref[:, TALL:WIDE] = jnp.zeros((MEMBERS, WIDE - TALL), F32)


def sum_kernel(m_ref, whole_ref, l_ref):
    mh, ml = split2(m_ref[...])
    l_ref[...] = dot(mh, whole_ref[...]) + dot(ml, whole_ref[...])


def finish(l_ref, prev_ref, next_ref, in_ref, c_ref, done=lambda at: None):
    halo = jnp.concatenate([prev_ref[...], next_ref[...]], axis=0)
    hh, hl = split2(jnp.transpose(halo)[0:TALL, :])
    mass = l_ref[ROWS:TALL, :] + dot(hh[ROWS:TALL], in_ref[...]) + dot(hl[ROWS:TALL], in_ref[...])
    inverse = 1.0 / mass[0:1, :]
    for at in CHUNKS:
        c_ref[at, :] = (l_ref[at, :] + dot(hh[at], in_ref[...]) + dot(hl[at], in_ref[...])) * inverse
        done(at)


CHUNKS = tuple(slice(a, a + 144) for a in range(0, ROWS, 144))


def storing(body, source, target, sems):
    copies = []

    def done(at):
        copies.append(pltpu.make_async_copy(source.at[at], target.at[at], sems.at[len(copies)]))
        copies[-1].start()

    body(done)
    for copy in copies:
        copy.wait()


def finish_kernel(l_ref, prev_ref, next_ref, in_ref, out_hbm, cur, sems):
    storing(lambda done: finish(l_ref, prev_ref, next_ref, in_ref, cur, done), cur, out_hbm, sems)


def next_kernel(l_ref, prev_ref, next_ref, in_ref, tend_ref, mrow_ref, dx_ref, dy_ref, out_ref,
                m_ref, north_ref, south_ref, cur, dxs, dys):
    finish(l_ref, prev_ref, next_ref, in_ref, cur)
    move(lambda at, n: cur[pl.ds(at, n), :], tend_ref, mrow_ref, dx_ref, dy_ref, out_ref,
         dxs, dys, m_ref, north_ref, south_ref)


def place_kernel(arrived_ref, out_hbm, cur, sems):
    rows = arrived_ref[...].reshape(COLS, WIDE)
    place_col = rows[:, ROWS:ROWS + 1]
    pick = jnp.where(iota((COLS, COLS), 1).astype(F32) == place_col, 1.0, 0.0).astype(BF16)
    hi, lo = split2(jnp.transpose(rows)[0:ROWS, :])

    def body(done):
        for at in CHUNKS:
            cur[at, :] = dot(hi[at], pick) + dot(lo[at], pick)
            done(at)

    storing(body, cur, out_hbm, sems)


def call(kernel, out, specs, scratch=(), semaphores=0, hbm_out=0):
    shapes = tuple((pltpu.HBM if k < hbm_out else pltpu.VMEM)(s, t) for k, (s, t) in enumerate(out))
    work = [pltpu.VMEM(s, t) for s, t in scratch]
    if semaphores:
        work.append(pltpu.SemaphoreType.DMA((semaphores,)))
    return pl.pallas_call(
        kernel, out_shape=shapes, in_specs=specs, out_specs=(HB,) * hbm_out + (VM,) * (len(out) - hbm_out),
        scratch_shapes=work, compiler_params=PARAMS)


def in_hbm(*arrays):
    return tuple(pltpu.with_memory_space_constraint(a, pltpu.HBM) for a in arrays)


def swapped(array, first):
    length = lax.axis_size(AXES)
    low = range(0 if first else 1, length, 2)
    pairs = [(i, (i + 1) % length) for i in low]
    return lax.ppermute(array, AXES, pairs + [(j, i) for i, j in pairs])


def step(state, metric, neighbours, cost_class, batch_slot, level_mix, field_coupling_matrix):
    me = lax.axis_index(AXES).astype(jnp.int32).reshape(1)
    base = me * MEMBERS
    state2 = state.reshape(ROWS, COLS)
    dx, dy = (jnp.asarray(a) for a in derivative_blocks())
    send, tend, m, mine_a, mine_b, out_rows, in_rows, mrow = physics_call(
        state2, cost_class, batch_slot, level_mix, field_coupling_matrix, me, metric, neighbours, dx, dy)
    (whole,) = call(whole_kernel, [((COLS, COLS), BF16)], [SM, VM])(base, neighbours)
    arrived = lax.all_to_all(send, AXES, split_axis=0, concat_axis=0, tiled=True)
    for substep in range(SUBSTEPS):
        theirs_b = swapped(mine_b, False)
        theirs_a = swapped(mine_a, True)
        (total,) = call(sum_kernel, [MOVED], [VM, VM])(m, whole)
        if substep < SUBSTEPS - 1:
            m, mine_a, mine_b = call(next_kernel, [MOVED, HALO, HALO], [VM] * 9, [GRID] * 3)(
                total, theirs_a, theirs_b, in_rows, tend, mrow, dx, dy, out_rows)
    (physics_state,) = call(place_kernel, [GRID], [VM], [GRID], len(CHUNKS), 1)(arrived)
    (state_out,) = call(finish_kernel, [GRID], [VM] * 4, [GRID], len(CHUNKS), 1)(
        total, theirs_a, theirs_b, in_rows)
    return state_out.reshape(state.shape), physics_state.reshape(state.shape)


def solution(mesh):
    split = P(None, AXES)
    whole = P(None, None, AXES)
    return jax.shard_map(
        step, mesh=mesh, in_specs=(whole, split, split, split, P(), P(), P()),
        out_specs=(whole, whole), check_vma=False)
```

```python
import jax
import jax.numpy as jnp
import numpy as np
from jax import lax
from jax.experimental import pallas as pl
from jax.experimental.pallas import tpu as pltpu
from jax.sharding import PartitionSpec as P


AXES = ("elem", "face")
F32 = jnp.float32
BF16 = jnp.bfloat16
HIGHEST = lax.Precision.HIGHEST
FIELDS, LEVELS, SUBSTEPS = 10, 72, 3
ROWS, COLS, MEMBERS, WIDE = 720, 512, 32, 768
TALL = ROWS + 8
PHYSICS_RATE, TIME_STEP = 0.1, 0.02
VM = pl.BlockSpec(memory_space=pltpu.VMEM)
HB = pl.BlockSpec(memory_space=pltpu.HBM)
SM = pl.BlockSpec(memory_space=pltpu.SMEM)
PARAMS = pltpu.CompilerParams(vmem_limit_bytes=30 << 20)


def gll_matrix():
    nodes = np.array([-1.0, -1.0 / np.sqrt(5.0), 1.0 / np.sqrt(5.0), 1.0])
    derivative = np.zeros((4, 4))
    for i in range(4):
        for j in range(4):
            others = [k for k in range(4) if k != j]
            if i == j:
                derivative[i, j] = sum(1.0 / (nodes[j] - nodes[k]) for k in others)
            else:
                top = np.prod([nodes[i] - nodes[k] for k in others if k != i])
                derivative[i, j] = top / np.prod([nodes[j] - nodes[k] for k in others])
    return derivative


def derivative_blocks():
    d = gll_matrix()
    across = np.kron(np.eye(4), d).astype(np.float32).T
    upward = np.kron(d, np.eye(4)).astype(np.float32).T
    return np.kron(np.eye(16), across).astype(np.float32), np.kron(np.eye(16), upward).astype(np.float32)


def split2(v):
    hi = v.astype(BF16)
    return hi, (v - hi.astype(F32)).astype(BF16)


def dot(a, b):
    return jnp.dot(a, b, preferred_element_type=F32)


def dot_nt(a, b):
    return lax.dot_general(a, b, (((1,), (1,)), ((), ())), preferred_element_type=F32)


def iota(shape, dim):
    return lax.broadcasted_iota(jnp.int32, shape, dim)


def expand_points(table):
    spread = jnp.where(iota((32, COLS), 1) // 16 == iota((32, COLS), 0), 1.0, 0.0)
    wide = jnp.dot(table, spread, precision=HIGHEST, preferred_element_type=F32)
    wide = jnp.where(iota((16, COLS), 1) % 16 == iota((16, COLS), 0), wide, 0.0)
    return jnp.sum(wide, axis=0, keepdims=True)


def as_column(row):
    return jnp.transpose(jnp.broadcast_to(row, (8, COLS)))[:, 0:1]


def rank_row(key_row):
    key_col = as_column(key_row)
    return jnp.sum(jnp.where(key_col < key_row, 1.0, 0.0), axis=0, keepdims=True)


HALF = COLS // 2
SIZES = (32, 96, 128, 160, HALF)


def all_started(*copies):
    for copy in copies:
        copy.start()
    return copies


def copies(pairs, sems):
    return all_started(*(pltpu.make_async_copy(a, b, sems.at[k]) for k, (a, b) in enumerate(pairs)))


def sweeps(x_ref, kk, yy, tt, rr, qa, qb, cls, lanes):
    n1, n2, n3 = (jnp.sum(jnp.where(lanes & (cls > j + 0.5), 1, 0)) for j in (1, 2, 3))
    xh, xl = split2(x_ref[...])
    xhh = jnp.concatenate([xh, xh], axis=1)
    y = (dot(xl, kk[0:WIDE, :]) + dot(xhh, kk[...])) * (1.0 / PHYSICS_RATE)
    yy[...] = y
    t = jnp.tanh(y)
    tt[...] = t
    q = t.astype(BF16)
    rr[...] = t - q.astype(F32)
    qa[...] = q

    def step(rows, live, old, new, low):
        deep = 2 * WIDE if low else WIDE
        acc = dot(old[0:rows, 0:deep], kk[0:deep, :])
        for b in range(0, rows, 32):
            rb = slice(b, b + 32)
            y = yy[rb, :] + acc[rb]
            yy[rb, :] = y
            t = jnp.tanh(y)
            if b + 32 > max((0,) + tuple(n for n in SIZES if n < rows)):
                tt[rb, :] += jnp.where(iota((32, WIDE), 0) + b < live, t, 0.0)
            else:
                tt[rb, :] += t
            s = t + rr[rb, :]
            q = s.astype(BF16)
            rr[rb, :] = s - q.astype(F32)
            new[rb, 0:WIDE] = q
            if not low:
                new[rb, WIDE:] = (old[rb, :].astype(F32) + q.astype(F32)).astype(BF16)

    def sweep(k, old, new, low):
        live = jnp.where(k < 4, HALF, jnp.where(k < 8, n1, jnp.where(k < 12, n2, jnp.where(k < 16, n3, 0))))
        for below, rows in zip((0,) + SIZES, SIZES):
            @pl.when((live > below) & (live <= rows))
            def _():
                step(rows, live, old, new, low)

    def two_sweeps(j, _):
        sweep(2 * j + 1, qa, qb, False)
        sweep(2 * j + 2, qb, qa, True)
        return 0

    lax.fori_loop(0, 8, two_sweeps, 0)


def sent(x, ranks):
    pick = jnp.where(iota((HALF, HALF), 0).astype(F32) == ranks, 1.0, 0.0).astype(BF16)
    hi, lo = split2(x)
    return (dot(pick, hi) + dot(pick, lo)).reshape(HALF // 2, 2, WIDE)


def part1_kernel(me_ref, fcm_hbm, state_hbm, class_hbm, slots_hbm, mix_hbm,
                 send_hbm, x2_hbm, kk_hbm, perm_hbm, t1_hbm, info_hbm,
                 k32, kk, state_ref, class_ref, slot_ref, mix_ref, x0, yy, tt, rr, qa, qb, send_ref, pp, info,
                 fcm_ref, sems, out_sems):
    me = me_ref[0]
    load_fcm, load_mix, load_slots, load_class, load_state = copies(
        ((fcm_hbm, fcm_ref), (mix_hbm, mix_ref),
         (slots_hbm.at[:, pl.ds(pl.multiple_of(me // 4 * 128, 128), 128)], slot_ref),
         (class_hbm, class_ref), (state_hbm, state_ref)), sems)
    rep = jnp.where(
        (iota((LEVELS, WIDE), 1) % LEVELS == iota((LEVELS, WIDE), 0)) & (iota((LEVELS, WIDE), 1) < ROWS), 1.0, 0.0
    ).astype(BF16)
    lane = iota((1, WIDE), 1)
    load_fcm.wait()
    load_mix.wait()
    for f in range(FIELDS):
        crow = jnp.zeros((1, WIDE), F32)
        for g in range(FIELDS):
            crow = jnp.where((lane >= LEVELS * g) & (lane < LEVELS * g + LEVELS), PHYSICS_RATE * fcm_ref[g, f], crow)
        mh, ml = split2(jnp.transpose(mix_ref[f]))
        k32[LEVELS * f:LEVELS * f + LEVELS, :] = (dot(mh, rep) + dot(ml, rep)) * crow
    k32[ROWS:WIDE, :] = jnp.zeros((WIDE - ROWS, WIDE), F32)
    hi, lo = split2(k32[...])
    kk[0:WIDE, :] = hi
    kk[WIDE:, :] = lo
    store_kk = pltpu.make_async_copy(kk, kk_hbm, out_sems.at[0])
    store_kk.start()
    load_slots.wait()
    load_class.wait()
    part = me % 4
    own = slot_ref[:, 0:MEMBERS]
    for j in range(1, 4):
        own = jnp.where(part == j, slot_ref[:, MEMBERS * j:MEMBERS * j + MEMBERS], own)
    cls = expand_points(class_ref[...].astype(F32))
    slot = expand_points(own.astype(F32))
    col = iota((1, COLS), 1).astype(F32)
    srank = rank_row(slot)
    batch = jnp.floor(srank * 0.25)
    within = srank - 4.0 * batch
    late = within < 1.5
    hrank = 2.0 * batch + jnp.where(late, within, within - 2.0)
    crank = rank_row(jnp.where(late, 4.0 * COLS, 0.0) + (4.0 - cls) * COLS + col)
    place = slot - jnp.floor(slot * (1.0 / COLS)) * COLS
    perm = jnp.where(iota((COLS, COLS), 0).astype(F32) == crank, 1.0, 0.0).astype(BF16)
    pp[...] = perm
    store_perm = pltpu.make_async_copy(pp, perm_hbm, out_sems.at[1])
    store_perm.start()
    row16 = iota((16, COLS), 0)
    notes = jnp.where(row16 == 0, hrank, jnp.where(row16 == 1, cls, 0.0)).astype(BF16)
    info[...] = dot_nt(notes, perm)[0:8, :]
    store_info = pltpu.make_async_copy(info, info_hbm, out_sems.at[2])
    store_info.start()
    extra = jnp.where(iota((128, COLS), 0) == 0, place, 0.0)
    eh, el = split2(extra)
    x0[:, ROWS:WIDE] = (dot_nt(perm, eh) + dot_nt(perm, el))[:, 0:WIDE - ROWS]
    load_state.wait()
    sh, sl = split2(state_ref[...])
    x0[:, 0:ROWS] = dot_nt(perm, sh) + dot_nt(perm, sl)
    store_x2 = pltpu.make_async_copy(x0.at[HALF:COLS], x2_hbm, out_sems.at[3])
    store_x2.start()
    sweeps(x0.at[0:HALF], kk, yy, tt, rr, qa, qb, info[1:2, :], iota((1, COLS), 1) < HALF)
    store_t1 = pltpu.make_async_copy(tt, t1_hbm, out_sems.at[4])
    store_t1.start()
    send_ref[...] = sent(x0[0:HALF, :] + PHYSICS_RATE * tt[...], info[0:1, 0:HALF])
    pltpu.sync_copy(send_ref, send_hbm)
    for store in (store_kk, store_perm, store_info, store_x2, store_t1):
        store.wait()


def part2_kernel(me_ref, x2_hbm, kk_hbm, perm_hbm, t1_hbm, info_hbm, state_hbm, metric_hbm, nb_hbm, dx_hbm, dy_hbm,
                 send_hbm, tend_ref, m_ref, mine_a_ref, mine_b_ref, out_ref, in_ref, mrow_ref,
                 x2, kk, pp, t1, info, state_ref, metric_ref, nb_ref, dx_ref, dy_ref,
                 yy, tt, rr, qa, qb, send_ref, dxs, dys, sems):
    me = me_ref[0]
    loads = copies(((info_hbm, info), (x2_hbm, x2), (kk_hbm, kk), (perm_hbm, pp), (t1_hbm, t1), (state_hbm, state_ref),
                    (metric_hbm, metric_ref), (nb_hbm, nb_ref), (dx_hbm, dx_ref), (dy_hbm, dy_ref)), sems)
    for load in loads[0:3]:
        load.wait()
    sweeps(x2, kk, yy, tt, rr, qa, qb, info[1:2, :], iota((1, COLS), 1) >= HALF)
    send_ref[...] = sent(x2[...] + PHYSICS_RATE * tt[...], info[0:1, HALF:COLS])
    store_send = pltpu.make_async_copy(send_ref, send_hbm, sems.at[10])
    store_send.start()
    for load in loads[3:]:
        load.wait()
    ah, al = split2(jnp.transpose(t1[...])[0:ROWS, :] * (PHYSICS_RATE / SUBSTEPS))
    bh, bl = split2(jnp.transpose(tt[...])[0:ROWS, :] * (PHYSICS_RATE / SUBSTEPS))
    first, second = pp[0:HALF, :], pp[HALF:COLS, :]
    tend_ref[...] = (dot(ah, first) + dot(al, first)) + (dot(bh, second) + dot(bl, second))
    tables(me * MEMBERS, nb_ref, metric_ref, out_ref, in_ref, mrow_ref)
    move(lambda at, n: state_ref[pl.ds(at, n), :], tend_ref, mrow_ref, dx_ref, dy_ref, out_ref,
         dxs, dys, m_ref, mine_a_ref, mine_b_ref)
    store_send.wait()


HALO = ((MEMBERS, WIDE), F32)
MOVED = ((TALL, COLS), F32)
GRID = ((ROWS, COLS), F32)
SEND = ((HALF // 2, 2, WIDE), F32)
HALF_X = ((HALF, WIDE), F32)
OPERATOR = ((2 * WIDE, WIDE), BF16)
PERM = ((COLS, COLS), BF16)
INFO = ((8, COLS), F32)
SWEEP = [HALF_X, HALF_X, HALF_X, ((HALF, WIDE), BF16), ((HALF, 2 * WIDE), BF16), SEND]


def element_tables(neighbours_ref, base):
    local = neighbours_ref[...] - base
    outside = (local < 0) | (local >= MEMBERS)
    wide = jnp.concatenate([local.astype(F32), jnp.where(outside, 1.0, 0.0)], axis=0)
    spread = jnp.where(iota((MEMBERS, COLS), 1) // 16 == iota((MEMBERS, COLS), 0), 1.0, 0.0)
    by_column = jnp.dot(wide, spread, precision=HIGHEST, preferred_element_type=F32)
    return wide, by_column, spread


def east_west(by_column):
    col = iota((1, COLS), 1)
    ix, line = col % 4, (col % 16) // 4 * 4
    source = jnp.where(ix == 3, 16.0 * by_column[0:1] + line.astype(F32),
                       jnp.where(ix == 0, 16.0 * by_column[1:2] + (line + 3).astype(F32), -1.0))
    row = iota((COLS, COLS), 0)
    hit = (row.astype(F32) == source) | (row == iota((COLS, COLS), 1))
    return jnp.where(hit, 1.0, 0.0).astype(BF16)


def north_south(by_column):
    col = iota((1, COLS), 1)
    ix, iy = (col % 4).astype(F32), (col % 16) // 4
    north = jnp.where(by_column[6:7] > 0.5, -1.0, 16.0 * by_column[2:3] + ix)
    south = jnp.where(by_column[7:8] > 0.5, -1.0, 16.0 * by_column[3:4] + 12.0 + ix)
    source = jnp.where(iy == 3, north, jnp.where(iy == 0, south, -1.0))
    row = iota((COLS, COLS), 0)
    hit = (row.astype(F32) == source) | (row == iota((COLS, COLS), 1))
    return jnp.where(hit, 1.0, 0.0).astype(BF16)


def rank_among(key, member, spread):
    key8 = jnp.broadcast_to(jnp.where(member > 0.5, key, 1e9), (8, MEMBERS))
    key_col = jnp.transpose(key8)[:, 0:1]
    rank = jnp.sum(jnp.where(key_col < key, 1.0, 0.0), axis=0, keepdims=True)
    return jnp.dot(jnp.broadcast_to(rank, (8, MEMBERS)), spread, precision=HIGHEST,
                   preferred_element_type=F32)[0:1]


def halo_targets(wide, by_column, spread):
    col = iota((1, COLS), 1)
    ix, iy = (col % 4).astype(F32), (col % 16) // 4
    own = iota((1, MEMBERS), 1).astype(F32)
    up, down = by_column[6:7] > 0.5, by_column[7:8] > 0.5
    to_north = jnp.where((iy == 3) & up, 8.0 * ix + rank_among(own, wide[6:7], spread), -1.0)
    to_south = jnp.where((iy == 0) & down, 8.0 * ix + rank_among(own, wide[7:8], spread), -1.0)
    from_south = jnp.where((iy == 0) & down, 8.0 * ix + rank_among(wide[3:4], wide[7:8], spread), -1.0)
    from_north = jnp.where((iy == 3) & up, 8.0 * ix + rank_among(wide[2:3], wide[6:7], spread), -1.0)
    return to_north, to_south, from_south, from_north


def two_selections(first, second):
    row = iota((2 * MEMBERS, COLS), 0).astype(F32)
    hit = (row == first) | ((row - MEMBERS == second) & (second > -0.5))
    return jnp.where(hit, 1.0, 0.0).astype(BF16)


def whole_kernel(base_ref, neighbours_ref, whole_ref):
    base = base_ref[0]
    _, by_column, _ = element_tables(neighbours_ref, base)
    whole_ref[...] = dot(east_west(by_column), north_south(by_column)).astype(BF16)


def tables(base, neighbours_ref, metric_ref, out_ref, in_ref, mrow_ref):
    wide, by_column, spread = element_tables(neighbours_ref, base)
    to_north, to_south, from_south, from_north = halo_targets(wide, by_column, spread)
    odd = base // MEMBERS % 2 == 1
    sent = two_selections(jnp.where(odd, to_south, to_north), jnp.where(odd, to_north, to_south))
    out_ref[...] = dot_nt(sent, east_west(by_column)).astype(BF16)
    in_ref[...] = two_selections(jnp.where(odd, from_south, from_north), jnp.where(odd, from_north, from_south))
    mrow_ref[...] = jnp.broadcast_to(expand_points(metric_ref[...]), (8, COLS))


def move(read, tend_ref, mrow_ref, dx_ref, dy_ref, out_ref, dxs, dys, m_ref, north_ref, south_ref):
    vh, vl = split2(read(0, ROWS))
    for half in (0, 256):
        at = slice(half, half + 256)
        for d_ref, acc in ((dx_ref, dxs), (dy_ref, dys)):
            dh, dl = split2(d_ref[...])
            acc[:, at] = dot(vh[:, at], dh) + dot(vl[:, at], dh) + dot(vh[:, at], dl)
    metric = mrow_ref[0:1, :]
    u, v = read(0, LEVELS), read(LEVELS, LEVELS)
    for f in range(FIELDS):
        at = pl.ds(LEVELS * f, LEVELS)
        rate = u * dxs[at, :] + v * dys[at, :]
        m_ref[at, :] = metric * ((read(LEVELS * f, LEVELS) - TIME_STEP * rate) + tend_ref[at, :])
    m_ref[ROWS:TALL, :] = mrow_ref[...]
    mh, ml = split2(m_ref[...])
    halo = dot_nt(out_ref[...], mh) + dot_nt(out_ref[...], ml)
    north_ref[:, 0:TALL] = halo[0:MEMBERS]
    south_ref[:, 0:TALL] = halo[MEMBERS:]
    north_ref[:, TALL:WIDE] = jnp.zeros((MEMBERS, WIDE - TALL), F32)
    south_ref[:, TALL:WIDE] = jnp.zeros((MEMBERS, WIDE - TALL), F32)


def sum_kernel(m_ref, whole_ref, l_ref):
    mh, ml = split2(m_ref[...])
    l_ref[...] = dot(mh, whole_ref[...]) + dot(ml, whole_ref[...])


def finish(l_ref, prev_ref, next_ref, in_ref, c_ref, done=lambda at: None):
    halo = jnp.concatenate([prev_ref[...], next_ref[...]], axis=0)
    hh, hl = split2(jnp.transpose(halo)[0:TALL, :])
    mass = l_ref[ROWS:TALL, :] + dot(hh[ROWS:TALL], in_ref[...]) + dot(hl[ROWS:TALL], in_ref[...])
    inverse = 1.0 / mass[0:1, :]
    for at in CHUNKS:
        c_ref[at, :] = (l_ref[at, :] + dot(hh[at], in_ref[...]) + dot(hl[at], in_ref[...])) * inverse
        done(at)


CHUNKS = tuple(slice(a, a + 144) for a in range(0, ROWS, 144))


def storing(body, source, target, sems):
    copies = []

    def done(at):
        copies.append(pltpu.make_async_copy(source.at[at], target.at[at], sems.at[len(copies)]))
        copies[-1].start()

    body(done)
    for copy in copies:
        copy.wait()


def finish_kernel(l_ref, prev_ref, next_ref, in_ref, out_hbm, cur, sems):
    storing(lambda done: finish(l_ref, prev_ref, next_ref, in_ref, cur, done), cur, out_hbm, sems)


def next_kernel(l_ref, prev_ref, next_ref, in_ref, tend_ref, mrow_ref, dx_ref, dy_ref, out_ref,
                m_ref, north_ref, south_ref, cur, dxs, dys):
    finish(l_ref, prev_ref, next_ref, in_ref, cur)
    move(lambda at, n: cur[pl.ds(at, n), :], tend_ref, mrow_ref, dx_ref, dy_ref, out_ref,
         dxs, dys, m_ref, north_ref, south_ref)


def place_kernel(first_ref, second_ref, out_hbm, cur, sems):
    rows = jnp.concatenate([first_ref[...].reshape(HALF, WIDE), second_ref[...].reshape(HALF, WIDE)], axis=0)
    place_col = rows[:, ROWS:ROWS + 1]
    pick = jnp.where(iota((COLS, COLS), 1).astype(F32) == place_col, 1.0, 0.0).astype(BF16)
    hi, lo = split2(jnp.transpose(rows)[0:ROWS, :])

    def body(done):
        for at in CHUNKS:
            cur[at, :] = dot(hi[at], pick) + dot(lo[at], pick)
            done(at)

    storing(body, cur, out_hbm, sems)


def call(kernel, out, specs, scratch=(), semaphores=(), hbm_out=0, smem=()):
    shapes = tuple((pltpu.HBM if k < hbm_out else pltpu.VMEM)(s, t) for k, (s, t) in enumerate(out))
    work = [pltpu.VMEM(s, t) for s, t in scratch] + [pltpu.SMEM(s, t) for s, t in smem]
    work += [pltpu.SemaphoreType.DMA((n,)) for n in semaphores]
    return pl.pallas_call(
        kernel, out_shape=shapes, in_specs=specs, out_specs=(HB,) * hbm_out + (VM,) * (len(out) - hbm_out),
        scratch_shapes=work, compiler_params=PARAMS)


def in_hbm(*arrays):
    return tuple(pltpu.with_memory_space_constraint(a, pltpu.HBM) for a in arrays)


def swapped(array, first):
    length = lax.axis_size(AXES)
    low = range(0 if first else 1, length, 2)
    pairs = [(i, (i + 1) % length) for i in low]
    return lax.ppermute(array, AXES, pairs + [(j, i) for i, j in pairs])


def step(state, metric, neighbours, cost_class, batch_slot, level_mix, field_coupling_matrix):
    me = lax.axis_index(AXES).astype(jnp.int32).reshape(1)
    base = me * MEMBERS
    state2 = state.reshape(ROWS, COLS)
    dx, dy = (jnp.asarray(a) for a in derivative_blocks())
    send1, *kept = call(
        part1_kernel, [SEND, HALF_X, OPERATOR, PERM, HALF_X, INFO], [SM] + [HB] * 5,
        [((WIDE, WIDE), F32), OPERATOR, GRID, ((16, MEMBERS), jnp.int32), ((16, 128), jnp.int32),
         ((FIELDS, LEVELS, LEVELS), F32), ((COLS, WIDE), F32)] + SWEEP + [PERM, INFO],
        [5, 5], 6, [((FIELDS, FIELDS), F32)],
    )(me, *in_hbm(field_coupling_matrix, state2, cost_class, batch_slot, level_mix))
    arrived1 = lax.all_to_all(send1, AXES, split_axis=0, concat_axis=0, tiled=True)
    send2, tend, m, mine_a, mine_b, out_rows, in_rows, mrow = call(
        part2_kernel,
        [SEND, GRID, MOVED, HALO, HALO, ((2 * MEMBERS, COLS), BF16), ((2 * MEMBERS, COLS), BF16), INFO],
        [SM] + [HB] * 10,
        [HALF_X, OPERATOR, PERM, HALF_X, INFO, GRID, ((16, MEMBERS), F32), ((4, MEMBERS), jnp.int32),
         ((256, 256), F32), ((256, 256), F32)] + SWEEP + [GRID, GRID],
        [11], 1,
    )(me, *in_hbm(*kept, state2, metric, neighbours, dx, dy))
    (whole,) = call(whole_kernel, [((COLS, COLS), BF16)], [SM, VM])(base, neighbours)
    arrived2 = lax.all_to_all(send2, AXES, split_axis=0, concat_axis=0, tiled=True)
    for substep in range(SUBSTEPS):
        theirs_b = swapped(mine_b, False)
        theirs_a = swapped(mine_a, True)
        (total,) = call(sum_kernel, [MOVED], [VM, VM])(m, whole)
        if substep < SUBSTEPS - 1:
            m, mine_a, mine_b = call(next_kernel, [MOVED, HALO, HALO], [VM] * 9, [GRID] * 3)(
                total, theirs_a, theirs_b, in_rows, tend, mrow, dx, dy, out_rows)
    (physics_state,) = call(place_kernel, [GRID], [VM, VM], [GRID], [len(CHUNKS)], 1)(arrived1, arrived2)
    (state_out,) = call(finish_kernel, [GRID], [VM] * 4, [GRID], [len(CHUNKS)], 1)(
        total, theirs_a, theirs_b, in_rows)
    return state_out.reshape(state.shape), physics_state.reshape(state.shape)


def solution(mesh):
    split = P(None, AXES)
    whole = P(None, None, AXES)
    return jax.shard_map(
        step, mesh=mesh, in_specs=(whole, split, split, split, P(), P(), P()),
        out_specs=(whole, whole), check_vma=False)
```

```python
from functools import partial

import jax
import jax.numpy as jnp
import numpy as np
from jax import lax
from jax.experimental import pallas as pl
from jax.experimental.pallas import tpu as pltpu
from jax.sharding import PartitionSpec as P


AXES = ("elem", "face")
F32 = jnp.float32
BF16 = jnp.bfloat16
HIGHEST = lax.Precision.HIGHEST
FIELDS, LEVELS, SUBSTEPS = 10, 72, 3
ROWS, COLS, MEMBERS, WIDE = 720, 512, 32, 768
TALL = ROWS + 8
PHYSICS_RATE, TIME_STEP = 0.1, 0.02
VM = pl.BlockSpec(memory_space=pltpu.VMEM)
HB = pl.BlockSpec(memory_space=pltpu.HBM)
SM = pl.BlockSpec(memory_space=pltpu.SMEM)
PARAMS = pltpu.CompilerParams(vmem_limit_bytes=30 << 20)


def gll_matrix():
    nodes = np.array([-1.0, -1.0 / np.sqrt(5.0), 1.0 / np.sqrt(5.0), 1.0])
    derivative = np.zeros((4, 4))
    for i in range(4):
        for j in range(4):
            others = [k for k in range(4) if k != j]
            if i == j:
                derivative[i, j] = sum(1.0 / (nodes[j] - nodes[k]) for k in others)
            else:
                top = np.prod([nodes[i] - nodes[k] for k in others if k != i])
                derivative[i, j] = top / np.prod([nodes[j] - nodes[k] for k in others])
    return derivative


def derivative_blocks():
    d = gll_matrix()
    across = np.kron(np.eye(4), d).astype(np.float32).T
    upward = np.kron(d, np.eye(4)).astype(np.float32).T
    return np.kron(np.eye(16), across).astype(np.float32), np.kron(np.eye(16), upward).astype(np.float32)


def split2(v):
    hi = v.astype(BF16)
    return hi, (v - hi.astype(F32)).astype(BF16)


def dot(a, b):
    return jnp.dot(a, b, preferred_element_type=F32)


def dot_nt(a, b):
    return lax.dot_general(a, b, (((1,), (1,)), ((), ())), preferred_element_type=F32)


def iota(shape, dim):
    return lax.broadcasted_iota(jnp.int32, shape, dim)


def expand_points(table):
    spread = jnp.where(iota((32, COLS), 1) // 16 == iota((32, COLS), 0), 1.0, 0.0)
    wide = jnp.dot(table, spread, precision=HIGHEST, preferred_element_type=F32)
    wide = jnp.where(iota((16, COLS), 1) % 16 == iota((16, COLS), 0), wide, 0.0)
    return jnp.sum(wide, axis=0, keepdims=True)


def as_column(row):
    return jnp.transpose(jnp.broadcast_to(row, (8, COLS)))[:, 0:1]


def rank_row(key_row):
    key_col = as_column(key_row)
    return jnp.sum(jnp.where(key_col < key_row, 1.0, 0.0), axis=0, keepdims=True)


LOCAL_SIZES = (160, 288, 416, COLS)
PIECES = ((0, 128, (64, 128)), (128, 320, (192,)), (320, 512, (192,)))


def all_started(*copies):
    for copy in copies:
        copy.start()
    return copies


def copies(pairs, sems):
    return all_started(*(pltpu.make_async_copy(a, b, sems.at[k]) for k, (a, b) in enumerate(pairs)))


def sweeps(x_ref, kk, yy, tt, rr, qa, qb, counts, sizes):
    n1, n2, n3 = counts
    xh, xl = split2(x_ref[...])
    xhh = jnp.concatenate([xh, xh], axis=1)
    y = (dot(xl, kk[0:WIDE, :]) + dot(xhh, kk[...])) * (1.0 / PHYSICS_RATE)
    yy[...] = y
    t = jnp.tanh(y)
    tt[...] = t
    q = t.astype(BF16)
    rr[...] = t - q.astype(F32)
    qa[...] = q

    def step(rows, live, old, new, low):
        deep = 2 * WIDE if low else WIDE
        acc = dot(old[0:rows, 0:deep], kk[0:deep, :])
        for b in range(0, rows, 32):
            rb = slice(b, b + 32)
            y = yy[rb, :] + acc[rb]
            yy[rb, :] = y
            t = jnp.tanh(y)
            if b + 32 > max((0,) + tuple(n for n in sizes if n < rows)):
                tt[rb, :] += jnp.where(iota((32, WIDE), 0) + b < live, t, 0.0)
            else:
                tt[rb, :] += t
            s = t + rr[rb, :]
            q = s.astype(BF16)
            rr[rb, :] = s - q.astype(F32)
            new[rb, 0:WIDE] = q
            if not low:
                new[rb, WIDE:] = (old[rb, :].astype(F32) + q.astype(F32)).astype(BF16)

    def sweep(k, old, new, low):
        live = jnp.where(k < 4, sizes[-1], jnp.where(k < 8, n1, jnp.where(k < 12, n2, jnp.where(k < 16, n3, 0))))
        for below, rows in zip((0,) + sizes, sizes):
            @pl.when((live > below) & (live <= rows))
            def _():
                step(rows, live, old, new, low)

    def two_sweeps(j, _):
        sweep(2 * j + 1, qa, qb, False)
        sweep(2 * j + 2, qb, qa, True)
        return 0

    lax.fori_loop(0, 8, two_sweeps, 0)


def sender_kernel(me_ref, state_hbm, class_hbm, slots_hbm, send_hbm, state_ref, class_ref, slot_ref, send_ref, sems):
    me = me_ref[0]
    load_slots, load_class, load_state = copies(
        ((slots_hbm.at[:, pl.ds(pl.multiple_of(me // 4 * 128, 128), 128)], slot_ref),
         (class_hbm, class_ref), (state_hbm, state_ref)), sems)
    load_slots.wait()
    load_class.wait()
    part = me % 4
    own = slot_ref[:, 0:MEMBERS]
    for j in range(1, 4):
        own = jnp.where(part == j, slot_ref[:, MEMBERS * j:MEMBERS * j + MEMBERS], own)
    cls = expand_points(class_ref[...].astype(F32))
    slot = expand_points(own.astype(F32))
    place = slot - jnp.floor(slot * (1.0 / COLS)) * COLS
    perm = jnp.where(iota((COLS, COLS), 0).astype(F32) == rank_row(slot), 1.0, 0.0).astype(BF16)
    row = iota((128, COLS), 0)
    eh, el = split2(jnp.where(row == 0, place, jnp.where(row == 1, cls, 0.0)))
    tail = dot_nt(perm, eh) + dot_nt(perm, el)
    load_state.wait()
    sh, sl = split2(state_ref[...])
    body = dot_nt(perm, sh) + dot_nt(perm, sl)
    send_ref[...] = jnp.concatenate([body, tail[:, 0:WIDE - ROWS]], axis=1).reshape(COLS // 4, 4, WIDE)
    pltpu.sync_copy(send_ref, send_hbm)


def physics_kernel(fcm_hbm, mix_hbm, class_hbm, state_hbm, kk_hbm, perm_hbm, tt,
                   mix_ref, class_ref, state_ref, k32, x0, yy, rr, qa, qb, pp, kk, fcm_ref, sems):
    loads = copies(((fcm_hbm, fcm_ref), (mix_hbm, mix_ref), (class_hbm, class_ref), (state_hbm, state_ref)), sems)
    rep = jnp.where(
        (iota((LEVELS, WIDE), 1) % LEVELS == iota((LEVELS, WIDE), 0)) & (iota((LEVELS, WIDE), 1) < ROWS), 1.0, 0.0
    ).astype(BF16)
    lane = iota((1, WIDE), 1)
    for load in loads[0:3]:
        load.wait()
    for f in range(FIELDS):
        crow = jnp.zeros((1, WIDE), F32)
        for g in range(FIELDS):
            crow = jnp.where((lane >= LEVELS * g) & (lane < LEVELS * g + LEVELS), PHYSICS_RATE * fcm_ref[g, f], crow)
        mh, ml = split2(jnp.transpose(mix_ref[f]))
        k32[LEVELS * f:LEVELS * f + LEVELS, :] = (dot(mh, rep) + dot(ml, rep)) * crow
    k32[ROWS:WIDE, :] = jnp.zeros((WIDE - ROWS, WIDE), F32)
    hi, lo = split2(k32[...])
    kk[0:WIDE, :] = hi
    kk[WIDE:, :] = lo
    store_kk = pltpu.make_async_copy(kk, kk_hbm, sems.at[4])
    store_kk.start()
    cls = expand_points(class_ref[...].astype(F32))
    crank = rank_row((4.0 - cls) * COLS + iota((1, COLS), 1).astype(F32))
    perm = jnp.where(iota((COLS, COLS), 0).astype(F32) == crank, 1.0, 0.0).astype(BF16)
    pp[...] = perm
    store_perm = pltpu.make_async_copy(pp, perm_hbm, sems.at[5])
    store_perm.start()
    for load in loads[3:]:
        load.wait()
    sh, sl = split2(state_ref[...])
    x0[:, 0:ROWS] = dot_nt(perm, sh) + dot_nt(perm, sl)
    x0[:, ROWS:WIDE] = jnp.zeros((COLS, WIDE - ROWS), F32)
    counts = tuple(jnp.sum(jnp.where(cls > j + 0.5, 1, 0)) for j in (1, 2, 3))
    sweeps(x0, kk, yy, tt, rr, qa, qb, counts, LOCAL_SIZES)
    store_kk.wait()
    store_perm.wait()


def start_kernel(me_ref, arrived_ref, tt, perm_hbm, nb_hbm, metric_hbm, dx_hbm, dy_hbm, state_hbm,
                 tend_ref, m_ref, mine_a_ref, mine_b_ref, out_ref, in_ref, mrow_ref,
                 pp, nb_ref, metric_ref, dx_ref, dy_ref, state_ref, dxs, dys, sems):
    me = me_ref[0]
    loads = copies(((perm_hbm, pp), (nb_hbm, nb_ref), (metric_hbm, metric_ref), (dx_hbm, dx_ref), (dy_hbm, dy_ref),
                    (state_hbm, state_ref)), sems)
    th, tl = split2(jnp.transpose(tt[...])[0:ROWS, :] * (PHYSICS_RATE / SUBSTEPS))
    for load in loads[0:3]:
        load.wait()
    tend_ref[...] = dot(th, pp[...]) + dot(tl, pp[...])
    tables(me * MEMBERS, nb_ref, metric_ref, out_ref, in_ref, mrow_ref)
    for load in loads[3:]:
        load.wait()
    move(lambda at, n: state_ref[pl.ds(at, n), :], tend_ref, mrow_ref, dx_ref, dy_ref, out_ref,
         dxs, dys, m_ref, mine_a_ref, mine_b_ref)


def piece(arrived_ref, kk, low, high, sizes, work):
    xs, yy, tt, rr, qa, qb = work
    rows = arrived_ref[...].reshape(COLS, WIDE)
    place_row = jnp.transpose(rows[:, WIDE - 128:WIDE])[ROWS - (WIDE - 128):ROWS - (WIDE - 128) + 1, :]
    pick = jnp.where((iota((high - low, COLS), 0) + low).astype(F32) == place_row, 1.0, 0.0).astype(BF16)
    hi, lo = split2(rows)
    xs[...] = dot(pick, hi) + dot(pick, lo)
    cls = xs[:, ROWS + 1:ROWS + 2]
    counts = tuple(jnp.sum(jnp.where(cls > j + 0.5, 1, 0)) for j in (1, 2, 3))
    sweeps(xs, kk, yy, tt, rr, qa, qb, counts, sizes)
    return xs[...] + PHYSICS_RATE * tt[...]


def piece_kernel(arrived_ref, kk, out_ref, *work, low, high, sizes):
    out_ref[...] = piece(arrived_ref, kk, low, high, sizes, work)


def last_kernel(arrived_ref, kk, first_ref, second_ref, out_hbm, cur, *work, low, high, sizes):
    sems = work[-1]
    last = piece(arrived_ref, kk, low, high, sizes, work[:-1])
    turned = jnp.transpose(jnp.concatenate([first_ref[...], second_ref[...], last], axis=0))

    def body(done):
        for at in CHUNKS:
            cur[at, :] = turned[at]
            done(at)

    storing(body, cur, out_hbm, sems)


def sweep_work(rows):
    tall = ((rows, WIDE), F32)
    return [tall] * 4 + [((rows, WIDE), BF16), ((rows, 2 * WIDE), BF16)]


HALO = ((MEMBERS, WIDE), F32)
MOVED = ((TALL, COLS), F32)
GRID = ((ROWS, COLS), F32)
SEND = ((COLS // 4, 4, WIDE), F32)
OPERATOR = ((2 * WIDE, WIDE), BF16)
PERM = ((COLS, COLS), BF16)
INFO = ((8, COLS), F32)
SELECT = ((2 * MEMBERS, COLS), BF16)
TABLE = ((16, MEMBERS), jnp.int32)


def element_tables(neighbours_ref, base):
    local = neighbours_ref[...] - base
    outside = (local < 0) | (local >= MEMBERS)
    wide = jnp.concatenate([local.astype(F32), jnp.where(outside, 1.0, 0.0)], axis=0)
    spread = jnp.where(iota((MEMBERS, COLS), 1) // 16 == iota((MEMBERS, COLS), 0), 1.0, 0.0)
    by_column = jnp.dot(wide, spread, precision=HIGHEST, preferred_element_type=F32)
    return wide, by_column, spread


def east_west(by_column):
    col = iota((1, COLS), 1)
    ix, line = col % 4, (col % 16) // 4 * 4
    source = jnp.where(ix == 3, 16.0 * by_column[0:1] + line.astype(F32),
                       jnp.where(ix == 0, 16.0 * by_column[1:2] + (line + 3).astype(F32), -1.0))
    row = iota((COLS, COLS), 0)
    hit = (row.astype(F32) == source) | (row == iota((COLS, COLS), 1))
    return jnp.where(hit, 1.0, 0.0).astype(BF16)


def north_south(by_column):
    col = iota((1, COLS), 1)
    ix, iy = (col % 4).astype(F32), (col % 16) // 4
    north = jnp.where(by_column[6:7] > 0.5, -1.0, 16.0 * by_column[2:3] + ix)
    south = jnp.where(by_column[7:8] > 0.5, -1.0, 16.0 * by_column[3:4] + 12.0 + ix)
    source = jnp.where(iy == 3, north, jnp.where(iy == 0, south, -1.0))
    row = iota((COLS, COLS), 0)
    hit = (row.astype(F32) == source) | (row == iota((COLS, COLS), 1))
    return jnp.where(hit, 1.0, 0.0).astype(BF16)


def rank_among(key, member, spread):
    key8 = jnp.broadcast_to(jnp.where(member > 0.5, key, 1e9), (8, MEMBERS))
    key_col = jnp.transpose(key8)[:, 0:1]
    rank = jnp.sum(jnp.where(key_col < key, 1.0, 0.0), axis=0, keepdims=True)
    return jnp.dot(jnp.broadcast_to(rank, (8, MEMBERS)), spread, precision=HIGHEST,
                   preferred_element_type=F32)[0:1]


def halo_targets(wide, by_column, spread):
    col = iota((1, COLS), 1)
    ix, iy = (col % 4).astype(F32), (col % 16) // 4
    own = iota((1, MEMBERS), 1).astype(F32)
    up, down = by_column[6:7] > 0.5, by_column[7:8] > 0.5
    to_north = jnp.where((iy == 3) & up, 8.0 * ix + rank_among(own, wide[6:7], spread), -1.0)
    to_south = jnp.where((iy == 0) & down, 8.0 * ix + rank_among(own, wide[7:8], spread), -1.0)
    from_south = jnp.where((iy == 0) & down, 8.0 * ix + rank_among(wide[3:4], wide[7:8], spread), -1.0)
    from_north = jnp.where((iy == 3) & up, 8.0 * ix + rank_among(wide[2:3], wide[6:7], spread), -1.0)
    return to_north, to_south, from_south, from_north


def two_selections(first, second):
    row = iota((2 * MEMBERS, COLS), 0).astype(F32)
    hit = (row == first) | ((row - MEMBERS == second) & (second > -0.5))
    return jnp.where(hit, 1.0, 0.0).astype(BF16)


def whole_kernel(base_ref, neighbours_ref, whole_ref):
    base = base_ref[0]
    _, by_column, _ = element_tables(neighbours_ref, base)
    whole_ref[...] = dot(east_west(by_column), north_south(by_column)).astype(BF16)


def tables(base, neighbours_ref, metric_ref, out_ref, in_ref, mrow_ref):
    wide, by_column, spread = element_tables(neighbours_ref, base)
    to_north, to_south, from_south, from_north = halo_targets(wide, by_column, spread)
    odd = base // MEMBERS % 2 == 1
    sent = two_selections(jnp.where(odd, to_south, to_north), jnp.where(odd, to_north, to_south))
    out_ref[...] = dot_nt(sent, east_west(by_column)).astype(BF16)
    in_ref[...] = two_selections(jnp.where(odd, from_south, from_north), jnp.where(odd, from_north, from_south))
    mrow_ref[...] = jnp.broadcast_to(expand_points(metric_ref[...]), (8, COLS))


def move(read, tend_ref, mrow_ref, dx_ref, dy_ref, out_ref, dxs, dys, m_ref, north_ref, south_ref):
    vh, vl = split2(read(0, ROWS))
    for half in (0, 256):
        at = slice(half, half + 256)
        for d_ref, acc in ((dx_ref, dxs), (dy_ref, dys)):
            dh, dl = split2(d_ref[...])
            acc[:, at] = dot(vh[:, at], dh) + dot(vl[:, at], dh) + dot(vh[:, at], dl)
    metric = mrow_ref[0:1, :]
    u, v = read(0, LEVELS), read(LEVELS, LEVELS)
    for f in range(FIELDS):
        at = pl.ds(LEVELS * f, LEVELS)
        rate = u * dxs[at, :] + v * dys[at, :]
        m_ref[at, :] = metric * ((read(LEVELS * f, LEVELS) - TIME_STEP * rate) + tend_ref[at, :])
    m_ref[ROWS:TALL, :] = mrow_ref[...]
    mh, ml = split2(m_ref[...])
    halo = dot_nt(out_ref[...], mh) + dot_nt(out_ref[...], ml)
    north_ref[:, 0:TALL] = halo[0:MEMBERS]
    south_ref[:, 0:TALL] = halo[MEMBERS:]
    north_ref[:, TALL:WIDE] = jnp.zeros((MEMBERS, WIDE - TALL), F32)
    south_ref[:, TALL:WIDE] = jnp.zeros((MEMBERS, WIDE - TALL), F32)


def sum_kernel(m_ref, whole_ref, l_ref):
    mh, ml = split2(m_ref[...])
    l_ref[...] = dot(mh, whole_ref[...]) + dot(ml, whole_ref[...])


def finish(l_ref, prev_ref, next_ref, in_ref, c_ref, done=lambda at: None):
    halo = jnp.concatenate([prev_ref[...], next_ref[...]], axis=0)
    hh, hl = split2(jnp.transpose(halo)[0:TALL, :])
    mass = l_ref[ROWS:TALL, :] + dot(hh[ROWS:TALL], in_ref[...]) + dot(hl[ROWS:TALL], in_ref[...])
    inverse = 1.0 / mass[0:1, :]
    for at in CHUNKS:
        c_ref[at, :] = (l_ref[at, :] + dot(hh[at], in_ref[...]) + dot(hl[at], in_ref[...])) * inverse
        done(at)


CHUNKS = tuple(slice(a, a + 144) for a in range(0, ROWS, 144))


def storing(body, source, target, sems):
    copies = []

    def done(at):
        copies.append(pltpu.make_async_copy(source.at[at], target.at[at], sems.at[len(copies)]))
        copies[-1].start()

    body(done)
    for copy in copies:
        copy.wait()


def finish_kernel(l_ref, prev_ref, next_ref, in_ref, out_hbm, cur, sems):
    storing(lambda done: finish(l_ref, prev_ref, next_ref, in_ref, cur, done), cur, out_hbm, sems)


def next_kernel(l_ref, prev_ref, next_ref, in_ref, tend_ref, mrow_ref, dx_ref, dy_ref, out_ref,
                m_ref, north_ref, south_ref, cur, dxs, dys):
    finish(l_ref, prev_ref, next_ref, in_ref, cur)
    move(lambda at, n: cur[pl.ds(at, n), :], tend_ref, mrow_ref, dx_ref, dy_ref, out_ref,
         dxs, dys, m_ref, north_ref, south_ref)


def call(kernel, out, specs, scratch=(), semaphores=(), hbm_out=0, smem=()):
    shapes = tuple((pltpu.HBM if k < hbm_out else pltpu.VMEM)(s, t) for k, (s, t) in enumerate(out))
    work = [pltpu.VMEM(s, t) for s, t in scratch] + [pltpu.SMEM(s, t) for s, t in smem]
    work += [pltpu.SemaphoreType.DMA((n,)) for n in semaphores]
    return pl.pallas_call(
        kernel, out_shape=shapes, in_specs=specs, out_specs=(HB,) * hbm_out + (VM,) * (len(out) - hbm_out),
        scratch_shapes=work, compiler_params=PARAMS)


def in_hbm(*arrays):
    return tuple(pltpu.with_memory_space_constraint(a, pltpu.HBM) for a in arrays)


def swapped(array, first):
    length = lax.axis_size(AXES)
    low = range(0 if first else 1, length, 2)
    pairs = [(i, (i + 1) % length) for i in low]
    return lax.ppermute(array, AXES, pairs + [(j, i) for i, j in pairs])


def step(state, metric, neighbours, cost_class, batch_slot, level_mix, field_coupling_matrix):
    me = lax.axis_index(AXES).astype(jnp.int32).reshape(1)
    base = me * MEMBERS
    state2 = state.reshape(ROWS, COLS)
    dx, dy = (jnp.asarray(a) for a in derivative_blocks())
    (send,) = call(
        sender_kernel, [SEND], [SM] + [HB] * 3, [GRID, TABLE, ((16, 128), jnp.int32), SEND], [3], 1,
    )(me, *in_hbm(state2, cost_class, batch_slot))
    arrived = lax.all_to_all(send, AXES, split_axis=0, concat_axis=0, tiled=True)
    kk, perm, sums = call(
        physics_kernel, [OPERATOR, PERM, ((COLS, WIDE), F32)], [HB] * 4,
        [((FIELDS, LEVELS, LEVELS), F32), TABLE, GRID, ((WIDE, WIDE), F32)] + sweep_work(COLS)[1:]
        + [PERM, OPERATOR],
        [6], 2, [((FIELDS, FIELDS), F32)],
    )(*in_hbm(field_coupling_matrix, level_mix, cost_class, state2))
    tend, m, mine_a, mine_b, out_rows, in_rows, mrow = call(
        start_kernel, [GRID, MOVED, HALO, HALO, SELECT, SELECT, INFO], [SM, VM, VM] + [HB] * 6,
        [PERM, ((4, MEMBERS), jnp.int32), ((16, MEMBERS), F32), ((256, 256), F32), ((256, 256), F32), GRID, GRID,
         GRID],
        [6],
    )(me, arrived, sums, *in_hbm(perm, neighbours, metric, dx, dy, state2))
    (whole,) = call(whole_kernel, [((COLS, COLS), BF16)], [SM, VM])(base, neighbours)
    done = []
    for substep in range(SUBSTEPS):
        theirs_b = swapped(mine_b, False)
        theirs_a = swapped(mine_a, True)
        (total,) = call(sum_kernel, [MOVED], [VM, VM])(m, whole)
        low, high, sizes = PIECES[substep]
        form = dict(low=low, high=high, sizes=sizes)
        if substep < SUBSTEPS - 1:
            done += call(
                partial(piece_kernel, **form), [((high - low, WIDE), F32)], [VM, VM],
                sweep_work(high - low))(arrived, kk)
        else:
            (physics_state,) = call(
                partial(last_kernel, **form), [GRID], [VM] * 4, [GRID] + sweep_work(high - low),
                [len(CHUNKS)], 1)(arrived, kk, *done)
        if substep < SUBSTEPS - 1:
            m, mine_a, mine_b = call(next_kernel, [MOVED, HALO, HALO], [VM] * 9, [GRID] * 3)(
                total, theirs_a, theirs_b, in_rows, tend, mrow, dx, dy, out_rows)
    (state_out,) = call(finish_kernel, [GRID], [VM] * 4, [GRID], [len(CHUNKS)], 1)(
        total, theirs_a, theirs_b, in_rows)
    return state_out.reshape(state.shape), physics_state.reshape(state.shape)


def solution(mesh):
    split = P(None, AXES)
    whole = P(None, None, AXES)
    return jax.shard_map(
        step, mesh=mesh, in_specs=(whole, split, split, split, P(), P(), P()),
        out_specs=(whole, whole), check_vma=False)
```

```python
import jax
import jax.numpy as jnp
import numpy as np
from jax import lax
from jax.experimental import pallas as pl
from jax.experimental.pallas import tpu as pltpu
from jax.sharding import PartitionSpec as P


AXES = ("elem", "face")
F32 = jnp.float32
BF16 = jnp.bfloat16
HIGHEST = lax.Precision.HIGHEST
FIELDS, LEVELS, SUBSTEPS = 10, 72, 3
ROWS, COLS, MEMBERS, WIDE = 720, 512, 32, 768
TALL = ROWS + 8
PHYSICS_RATE, TIME_STEP = 0.1, 0.02
VM = pl.BlockSpec(memory_space=pltpu.VMEM)
HB = pl.BlockSpec(memory_space=pltpu.HBM)
SM = pl.BlockSpec(memory_space=pltpu.SMEM)
PARAMS = pltpu.CompilerParams(vmem_limit_bytes=30 << 20)


def gll_matrix():
    nodes = np.array([-1.0, -1.0 / np.sqrt(5.0), 1.0 / np.sqrt(5.0), 1.0])
    derivative = np.zeros((4, 4))
    for i in range(4):
        for j in range(4):
            others = [k for k in range(4) if k != j]
            if i == j:
                derivative[i, j] = sum(1.0 / (nodes[j] - nodes[k]) for k in others)
            else:
                top = np.prod([nodes[i] - nodes[k] for k in others if k != i])
                derivative[i, j] = top / np.prod([nodes[j] - nodes[k] for k in others])
    return derivative


def derivative_blocks():
    d = gll_matrix()
    across = np.kron(np.eye(4), d).astype(np.float32).T
    upward = np.kron(d, np.eye(4)).astype(np.float32).T
    return np.kron(np.eye(16), across).astype(np.float32), np.kron(np.eye(16), upward).astype(np.float32)


SIZES = (160, 288, 416, COLS)


def split2(v):
    hi = v.astype(BF16)
    return hi, (v - hi.astype(F32)).astype(BF16)


def dot(a, b):
    return jnp.dot(a, b, preferred_element_type=F32)


def dot_nt(a, b):
    return lax.dot_general(a, b, (((1,), (1,)), ((), ())), preferred_element_type=F32)


def iota(shape, dim):
    return lax.broadcasted_iota(jnp.int32, shape, dim)


def expand_points(table):
    spread = jnp.where(iota((32, COLS), 1) // 16 == iota((32, COLS), 0), 1.0, 0.0)
    wide = jnp.dot(table, spread, precision=HIGHEST, preferred_element_type=F32)
    wide = jnp.where(iota((16, COLS), 1) % 16 == iota((16, COLS), 0), wide, 0.0)
    return jnp.sum(wide, axis=0, keepdims=True)


def as_column(row):
    return jnp.transpose(jnp.broadcast_to(row, (8, COLS)))[:, 0:1]


def rank_row(key_row):
    key_col = as_column(key_row)
    return jnp.sum(jnp.where(key_col < key_row, 1.0, 0.0), axis=0, keepdims=True)


def physics_kernel(me_ref, fcm_hbm, state_hbm, class_hbm, slots_hbm, mix_hbm, metric_hbm, nb_hbm, dx_hbm, dy_hbm,
                   send_hbm, tend_ref, m_ref, mine_a_ref, mine_b_ref, out_ref, in_ref, mrow_ref,
                   k32, kk, state_ref, class_ref, slot_ref, mix_ref, x0, yy, tt, rr, qa, qb, send_ref,
                   metric_ref, nb_ref, dx_ref, dy_ref, dxs, dys, fcm_ref, sems):
    me = me_ref[0]
    load_slots = pltpu.make_async_copy(
        slots_hbm.at[:, pl.ds(pl.multiple_of(me // 4 * 128, 128), 128)], slot_ref, sems.at[0])
    load_state = pltpu.make_async_copy(state_hbm, state_ref, sems.at[1])
    load_class = pltpu.make_async_copy(class_hbm, class_ref, sems.at[2])
    load_mix = pltpu.make_async_copy(mix_hbm, mix_ref, sems.at[3])
    load_fcm = pltpu.make_async_copy(fcm_hbm, fcm_ref, sems.at[4])
    load_metric = pltpu.make_async_copy(metric_hbm, metric_ref, sems.at[5])
    load_nb = pltpu.make_async_copy(nb_hbm, nb_ref, sems.at[6])
    load_dx = pltpu.make_async_copy(dx_hbm, dx_ref, sems.at[7])
    load_dy = pltpu.make_async_copy(dy_hbm, dy_ref, sems.at[8])
    load_fcm.start()
    load_mix.start()
    load_slots.start()
    load_class.start()
    load_state.start()
    load_nb.start()
    load_metric.start()
    load_dx.start()
    load_dy.start()
    rep = jnp.where(
        (iota((LEVELS, WIDE), 1) % LEVELS == iota((LEVELS, WIDE), 0)) & (iota((LEVELS, WIDE), 1) < ROWS), 1.0, 0.0
    ).astype(BF16)
    lane = iota((1, WIDE), 1)
    load_fcm.wait()
    load_mix.wait()
    for f in range(FIELDS):
        crow = jnp.zeros((1, WIDE), F32)
        for g in range(FIELDS):
            crow = jnp.where((lane >= LEVELS * g) & (lane < LEVELS * g + LEVELS), PHYSICS_RATE * fcm_ref[g, f], crow)
        mh, ml = split2(jnp.transpose(mix_ref[f]))
        k32[LEVELS * f:LEVELS * f + LEVELS, :] = (dot(mh, rep) + dot(ml, rep)) * crow
    k32[ROWS:WIDE, :] = jnp.zeros((WIDE - ROWS, WIDE), F32)
    hi, lo = split2(k32[...])
    kk[0:WIDE, :] = hi
    kk[WIDE:, :] = lo
    load_slots.wait()
    load_class.wait()
    part = me % 4
    own = slot_ref[:, 0:MEMBERS]
    for j in range(1, 4):
        own = jnp.where(part == j, slot_ref[:, MEMBERS * j:MEMBERS * j + MEMBERS], own)
    cls = expand_points(class_ref[...].astype(F32))
    slot = expand_points(own.astype(F32))
    col = iota((1, COLS), 1).astype(F32)
    crank = rank_row((4.0 - cls) * COLS + col)
    srank = rank_row(slot)
    place = slot - jnp.floor(slot * (1.0 / COLS)) * COLS
    perm = jnp.where(iota((COLS, COLS), 0).astype(F32) == crank, 1.0, 0.0).astype(BF16)
    extra = jnp.where(iota((128, COLS), 0) == 0, place, 0.0)
    eh, el = split2(extra)
    x0[:, ROWS:WIDE] = (dot_nt(perm, eh) + dot_nt(perm, el))[:, 0:WIDE - ROWS]
    rh, rl = split2(jnp.broadcast_to(srank, (16, COLS)))
    srank_sorted = (dot_nt(rh, perm) + dot_nt(rl, perm))[0:1, :]
    n1 = jnp.sum(jnp.where(cls > 1.5, 1, 0))
    n2 = jnp.sum(jnp.where(cls > 2.5, 1, 0))
    n3 = jnp.sum(jnp.where(cls > 3.5, 1, 0))
    load_state.wait()
    sh, sl = split2(state_ref[...])
    x0[:, 0:ROWS] = dot_nt(perm, sh) + dot_nt(perm, sl)
    xh, xl = split2(x0[...])
    xhh = jnp.concatenate([xh, xh], axis=1)
    for n in range(0, WIDE, 256):
        at = slice(n, n + 256)
        y = (dot(xl, kk[0:WIDE, at]) + dot(xhh, kk[:, at])) * (1.0 / PHYSICS_RATE)
        yy[:, at] = y
        t = jnp.tanh(y)
        tt[:, at] = t
        q = t.astype(BF16)
        rr[:, at] = t - q.astype(F32)
        qa[:, at] = q

    def step(rows, live, old, new, low):
        deep = 2 * WIDE if low else WIDE
        acc = dot(old[0:rows, 0:deep], kk[0:deep, :])
        for b in range(0, rows, 32):
            rb = slice(b, b + 32)
            y = yy[rb, :] + acc[rb]
            yy[rb, :] = y
            t = jnp.tanh(y)
            if b + 32 > max((0,) + tuple(n for n in SIZES if n < rows)):
                tt[rb, :] += jnp.where(iota((32, WIDE), 0) + b < live, t, 0.0)
            else:
                tt[rb, :] += t
            s = t + rr[rb, :]
            q = s.astype(BF16)
            rr[rb, :] = s - q.astype(F32)
            new[rb, 0:WIDE] = q
            if not low:
                new[rb, WIDE:] = (old[rb, 0:WIDE].astype(F32) + q.astype(F32)).astype(BF16)

    def sweep(k, old, new, low):
        live = jnp.where(k < 4, COLS, jnp.where(k < 8, n1, jnp.where(k < 12, n2, jnp.where(k < 16, n3, 0))))
        for below, rows in zip((0,) + SIZES, SIZES):
            @pl.when((live > below) & (live <= rows))
            def _():
                step(rows, live, old, new, low)

    def two_sweeps(j, _):
        sweep(2 * j + 1, qa, qb, False)
        sweep(2 * j + 2, qb, qa, True)
        return 0

    lax.fori_loop(0, 8, two_sweeps, 0)
    q_send = jnp.where(iota((COLS, COLS), 0).astype(F32) == srank_sorted, 1.0, 0.0).astype(BF16)
    fh, fl = split2(x0[...] + PHYSICS_RATE * tt[...])
    out = dot(q_send, fh) + dot(q_send, fl)
    send_ref[...] = out.reshape(COLS // 4, 4, WIDE)
    store_send = pltpu.make_async_copy(send_ref, send_hbm, sems.at[9])
    store_send.start()
    th, tl = split2(jnp.transpose(tt[...])[0:ROWS, :] * (PHYSICS_RATE / SUBSTEPS))
    tend_ref[...] = dot(th, perm) + dot(tl, perm)
    load_nb.wait()
    load_metric.wait()
    tables(me * MEMBERS, nb_ref, metric_ref, out_ref, in_ref, mrow_ref)
    load_dx.wait()
    load_dy.wait()
    move(lambda at, n: state_ref[pl.ds(at, n), :], tend_ref, mrow_ref, dx_ref, dy_ref, out_ref,
         dxs, dys, m_ref, mine_a_ref, mine_b_ref)
    store_send.wait()


HALO = ((MEMBERS, WIDE), F32)
MOVED = ((TALL, COLS), F32)
GRID = ((ROWS, COLS), F32)


def physics_call(state2, cost_class, batch_slot, level_mix, fcm, me, metric, neighbours, dx, dy):
    work = [((WIDE, WIDE), F32), ((2 * WIDE, WIDE), BF16), GRID, ((16, MEMBERS), jnp.int32),
            ((16, 128), jnp.int32), ((FIELDS, LEVELS, LEVELS), F32)]
    work += [((COLS, WIDE), F32)] * 4 + [((COLS, WIDE), BF16), ((COLS, 2 * WIDE), BF16), ((COLS // 4, 4, WIDE), F32)]
    work += [((16, MEMBERS), F32), ((4, MEMBERS), jnp.int32), ((256, 256), F32), ((256, 256), F32), GRID, GRID]
    out = [((COLS // 4, 4, WIDE), F32), GRID, MOVED, HALO, HALO, ((2 * MEMBERS, COLS), BF16),
           ((2 * MEMBERS, COLS), BF16), ((8, COLS), F32)]
    shapes = tuple((pltpu.HBM if k < 1 else pltpu.VMEM)(s, t) for k, (s, t) in enumerate(out))
    return pl.pallas_call(
        physics_kernel, out_shape=shapes, in_specs=[SM] + [HB] * 9, out_specs=(HB,) + (VM,) * 7,
        scratch_shapes=[pltpu.VMEM(s, t) for s, t in work]
        + [pltpu.SMEM((FIELDS, FIELDS), F32), pltpu.SemaphoreType.DMA((10,))],
        compiler_params=PARAMS, name="physics",
    )(me, *in_hbm(fcm, state2, cost_class, batch_slot, level_mix, metric, neighbours, dx, dy))


def element_tables(neighbours_ref, base):
    local = neighbours_ref[...] - base
    outside = (local < 0) | (local >= MEMBERS)
    wide = jnp.concatenate([local.astype(F32), jnp.where(outside, 1.0, 0.0)], axis=0)
    spread = jnp.where(iota((MEMBERS, COLS), 1) // 16 == iota((MEMBERS, COLS), 0), 1.0, 0.0)
    by_column = jnp.dot(wide, spread, precision=HIGHEST, preferred_element_type=F32)
    return wide, by_column, spread


def east_west(by_column):
    col = iota((1, COLS), 1)
    ix, line = col % 4, (col % 16) // 4 * 4
    source = jnp.where(ix == 3, 16.0 * by_column[0:1] + line.astype(F32),
                       jnp.where(ix == 0, 16.0 * by_column[1:2] + (line + 3).astype(F32), -1.0))
    row = iota((COLS, COLS), 0)
    hit = (row.astype(F32) == source) | (row == iota((COLS, COLS), 1))
    return jnp.where(hit, 1.0, 0.0).astype(BF16)


def north_south(by_column):
    col = iota((1, COLS), 1)
    ix, iy = (col % 4).astype(F32), (col % 16) // 4
    north = jnp.where(by_column[6:7] > 0.5, -1.0, 16.0 * by_column[2:3] + ix)
    south = jnp.where(by_column[7:8] > 0.5, -1.0, 16.0 * by_column[3:4] + 12.0 + ix)
    source = jnp.where(iy == 3, north, jnp.where(iy == 0, south, -1.0))
    row = iota((COLS, COLS), 0)
    hit = (row.astype(F32) == source) | (row == iota((COLS, COLS), 1))
    return jnp.where(hit, 1.0, 0.0).astype(BF16)


def rank_among(key, member, spread):
    key8 = jnp.broadcast_to(jnp.where(member > 0.5, key, 1e9), (8, MEMBERS))
    key_col = jnp.transpose(key8)[:, 0:1]
    rank = jnp.sum(jnp.where(key_col < key, 1.0, 0.0), axis=0, keepdims=True)
    return jnp.dot(jnp.broadcast_to(rank, (8, MEMBERS)), spread, precision=HIGHEST,
                   preferred_element_type=F32)[0:1]


def halo_targets(wide, by_column, spread):
    col = iota((1, COLS), 1)
    ix, iy = (col % 4).astype(F32), (col % 16) // 4
    own = iota((1, MEMBERS), 1).astype(F32)
    up, down = by_column[6:7] > 0.5, by_column[7:8] > 0.5
    to_north = jnp.where((iy == 3) & up, 8.0 * ix + rank_among(own, wide[6:7], spread), -1.0)
    to_south = jnp.where((iy == 0) & down, 8.0 * ix + rank_among(own, wide[7:8], spread), -1.0)
    from_south = jnp.where((iy == 0) & down, 8.0 * ix + rank_among(wide[3:4], wide[7:8], spread), -1.0)
    from_north = jnp.where((iy == 3) & up, 8.0 * ix + rank_among(wide[2:3], wide[6:7], spread), -1.0)
    return to_north, to_south, from_south, from_north


def two_selections(first, second):
    row = iota((2 * MEMBERS, COLS), 0).astype(F32)
    hit = (row == first) | ((row - MEMBERS == second) & (second > -0.5))
    return jnp.where(hit, 1.0, 0.0).astype(BF16)


def whole_kernel(base_ref, neighbours_ref, whole_ref):
    base = base_ref[0]
    _, by_column, _ = element_tables(neighbours_ref, base)
    whole_ref[...] = dot(east_west(by_column), north_south(by_column)).astype(BF16)


def tables(base, neighbours_ref, metric_ref, out_ref, in_ref, mrow_ref):
    wide, by_column, spread = element_tables(neighbours_ref, base)
    to_north, to_south, from_south, from_north = halo_targets(wide, by_column, spread)
    odd = base // MEMBERS % 2 == 1
    sent = two_selections(jnp.where(odd, to_south, to_north), jnp.where(odd, to_north, to_south))
    out_ref[...] = dot_nt(sent, east_west(by_column)).astype(BF16)
    in_ref[...] = two_selections(jnp.where(odd, from_south, from_north), jnp.where(odd, from_north, from_south))
    mrow_ref[...] = jnp.broadcast_to(expand_points(metric_ref[...]), (8, COLS))


def move(read, tend_ref, mrow_ref, dx_ref, dy_ref, out_ref, dxs, dys, m_ref, north_ref, south_ref):
    vh, vl = split2(read(0, ROWS))
    for half in (0, 256):
        at = slice(half, half + 256)
        for d_ref, acc in ((dx_ref, dxs), (dy_ref, dys)):
            dh, dl = split2(d_ref[...])
            acc[:, at] = dot(vh[:, at], dh) + dot(vl[:, at], dh) + dot(vh[:, at], dl)
    metric = mrow_ref[0:1, :]
    u, v = read(0, LEVELS), read(LEVELS, LEVELS)
    for f in range(FIELDS):
        at = pl.ds(LEVELS * f, LEVELS)
        rate = u * dxs[at, :] + v * dys[at, :]
        m_ref[at, :] = metric * ((read(LEVELS * f, LEVELS) - TIME_STEP * rate) + tend_ref[at, :])
    m_ref[ROWS:TALL, :] = mrow_ref[...]
    mh, ml = split2(m_ref[...])
    halo = dot_nt(out_ref[...], mh) + dot_nt(out_ref[...], ml)
    north_ref[:, 0:TALL] = halo[0:MEMBERS]
    south_ref[:, 0:TALL] = halo[MEMBERS:]
    north_ref[:, TALL:WIDE] = jnp.zeros((MEMBERS, WIDE - TALL), F32)
    south_ref[:, TALL:WIDE] = jnp.zeros((MEMBERS, WIDE - TALL), F32)


def sum_kernel(m_ref, whole_ref, l_ref):
    mh, ml = split2(m_ref[...])
    l_ref[...] = dot(mh, whole_ref[...]) + dot(ml, whole_ref[...])


def finish(l_ref, prev_ref, next_ref, in_ref, c_ref, done=lambda at: None):
    halo = jnp.concatenate([prev_ref[...], next_ref[...]], axis=0)
    hh, hl = split2(jnp.transpose(halo)[0:TALL, :])
    mass = l_ref[ROWS:TALL, :] + dot(hh[ROWS:TALL], in_ref[...]) + dot(hl[ROWS:TALL], in_ref[...])
    inverse = 1.0 / mass[0:1, :]
    for at in CHUNKS:
        c_ref[at, :] = (l_ref[at, :] + dot(hh[at], in_ref[...]) + dot(hl[at], in_ref[...])) * inverse
        done(at)


CHUNKS = tuple(slice(a, a + 144) for a in range(0, ROWS, 144))


def storing(body, source, target, sems):
    copies = []

    def done(at):
        copies.append(pltpu.make_async_copy(source.at[at], target.at[at], sems.at[len(copies)]))
        copies[-1].start()

    body(done)
    for copy in copies:
        copy.wait()


def finish_kernel(l_ref, prev_ref, next_ref, in_ref, out_hbm, cur, sems):
    storing(lambda done: finish(l_ref, prev_ref, next_ref, in_ref, cur, done), cur, out_hbm, sems)


def next_kernel(l_ref, prev_ref, next_ref, in_ref, tend_ref, mrow_ref, dx_ref, dy_ref, out_ref,
                m_ref, north_ref, south_ref, cur, dxs, dys):
    finish(l_ref, prev_ref, next_ref, in_ref, cur)
    move(lambda at, n: cur[pl.ds(at, n), :], tend_ref, mrow_ref, dx_ref, dy_ref, out_ref,
         dxs, dys, m_ref, north_ref, south_ref)


def place_kernel(arrived_hbm, out_hbm, arrived_ref, cur, sems):
    pltpu.sync_copy(arrived_hbm, arrived_ref)
    rows = arrived_ref[...].reshape(COLS, WIDE)
    place_col = rows[:, ROWS:ROWS + 1]
    pick = jnp.where(iota((COLS, COLS), 1).astype(F32) == place_col, 1.0, 0.0).astype(BF16)
    hi, lo = split2(jnp.transpose(rows)[0:ROWS, :])

    def body(done):
        for at in CHUNKS:
            cur[at, :] = dot(hi[at], pick) + dot(lo[at], pick)
            done(at)

    storing(body, cur, out_hbm, sems)


def call(kernel, out, specs, scratch=(), semaphores=0, hbm_out=0):
    shapes = tuple((pltpu.HBM if k < hbm_out else pltpu.VMEM)(s, t) for k, (s, t) in enumerate(out))
    work = [pltpu.VMEM(s, t) for s, t in scratch]
    if semaphores:
        work.append(pltpu.SemaphoreType.DMA((semaphores,)))
    return pl.pallas_call(
        kernel, out_shape=shapes, in_specs=specs, out_specs=(HB,) * hbm_out + (VM,) * (len(out) - hbm_out),
        scratch_shapes=work, compiler_params=PARAMS)


def in_hbm(*arrays):
    return tuple(pltpu.with_memory_space_constraint(a, pltpu.HBM) for a in arrays)


def swapped(array, first):
    length = lax.axis_size(AXES)
    low = range(0 if first else 1, length, 2)
    pairs = [(i, (i + 1) % length) for i in low]
    return lax.ppermute(array, AXES, pairs + [(j, i) for i, j in pairs])


def step(state, metric, neighbours, cost_class, batch_slot, level_mix, field_coupling_matrix):
    me = lax.axis_index(AXES).astype(jnp.int32).reshape(1)
    base = me * MEMBERS
    state2 = state.reshape(ROWS, COLS)
    dx, dy = (jnp.asarray(a) for a in derivative_blocks())
    send, tend, m, mine_a, mine_b, out_rows, in_rows, mrow = physics_call(
        state2, cost_class, batch_slot, level_mix, field_coupling_matrix, me, metric, neighbours, dx, dy)
    (whole,) = call(whole_kernel, [((COLS, COLS), BF16)], [SM, VM])(base, neighbours)
    arrived = lax.all_to_all(send, AXES, split_axis=0, concat_axis=0, tiled=True)
    for substep in range(SUBSTEPS):
        theirs_b = swapped(mine_b, False)
        theirs_a = swapped(mine_a, True)
        (total,) = call(sum_kernel, [MOVED], [VM, VM])(m, whole)
        if substep < SUBSTEPS - 1:
            m, mine_a, mine_b = call(next_kernel, [MOVED, HALO, HALO], [VM] * 9, [GRID] * 3)(
                total, theirs_a, theirs_b, in_rows, tend, mrow, dx, dy, out_rows)
    (physics_state,) = call(place_kernel, [GRID], [HB], [((COLS // 4, 4, WIDE), F32), GRID], len(CHUNKS), 1)(
        *in_hbm(arrived))
    (state_out,) = call(finish_kernel, [GRID], [VM] * 4, [GRID], len(CHUNKS), 1)(
        total, theirs_a, theirs_b, in_rows)
    return state_out.reshape(state.shape), physics_state.reshape(state.shape)


def solution(mesh):
    split = P(None, AXES)
    whole = P(None, None, AXES)
    return jax.shard_map(
        step, mesh=mesh, in_specs=(whole, split, split, split, P(), P(), P()),
        out_specs=(whole, whole), check_vma=False)
```

```python
import jax
import jax.numpy as jnp
import numpy as np
from jax import lax
from jax.experimental import pallas as pl
from jax.experimental.pallas import tpu as pltpu
from jax.sharding import PartitionSpec as P


AXES = ("elem", "face")
F32 = jnp.float32
BF16 = jnp.bfloat16
HIGHEST = lax.Precision.HIGHEST
FIELDS, LEVELS, SUBSTEPS = 10, 72, 3
ROWS, COLS, MEMBERS, WIDE = 720, 512, 32, 768
TALL = ROWS + 8
PHYSICS_RATE, TIME_STEP = 0.1, 0.02
VM = pl.BlockSpec(memory_space=pltpu.VMEM)
HB = pl.BlockSpec(memory_space=pltpu.HBM)
SM = pl.BlockSpec(memory_space=pltpu.SMEM)
PARAMS = pltpu.CompilerParams(vmem_limit_bytes=30 << 20)


def gll_matrix():
    nodes = np.array([-1.0, -1.0 / np.sqrt(5.0), 1.0 / np.sqrt(5.0), 1.0])
    derivative = np.zeros((4, 4))
    for i in range(4):
        for j in range(4):
            others = [k for k in range(4) if k != j]
            if i == j:
                derivative[i, j] = sum(1.0 / (nodes[j] - nodes[k]) for k in others)
            else:
                top = np.prod([nodes[i] - nodes[k] for k in others if k != i])
                derivative[i, j] = top / np.prod([nodes[j] - nodes[k] for k in others])
    return derivative


def derivative_blocks():
    d = gll_matrix()
    across = np.kron(np.eye(4), d).astype(np.float32).T
    upward = np.kron(d, np.eye(4)).astype(np.float32).T
    return np.kron(np.eye(16), across).astype(np.float32), np.kron(np.eye(16), upward).astype(np.float32)


SIZES = (160, 288, 416, COLS)


def split2(v):
    hi = v.astype(BF16)
    return hi, (v - hi.astype(F32)).astype(BF16)


def dot(a, b):
    return jnp.dot(a, b, preferred_element_type=F32)


def dot_nt(a, b):
    return lax.dot_general(a, b, (((1,), (1,)), ((), ())), preferred_element_type=F32)


def iota(shape, dim):
    return lax.broadcasted_iota(jnp.int32, shape, dim)


def expand_points(table):
    spread = jnp.where(iota((32, COLS), 1) // 16 == iota((32, COLS), 0), 1.0, 0.0)
    wide = jnp.dot(table, spread, precision=HIGHEST, preferred_element_type=F32)
    wide = jnp.where(iota((16, COLS), 1) % 16 == iota((16, COLS), 0), wide, 0.0)
    return jnp.sum(wide, axis=0, keepdims=True)


def as_column(row):
    return jnp.transpose(jnp.broadcast_to(row, (8, COLS)))[:, 0:1]


def rank_row(key_row):
    key_col = as_column(key_row)
    return jnp.sum(jnp.where(key_col < key_row, 1.0, 0.0), axis=0, keepdims=True)


def physics_kernel(me_ref, fcm_hbm, state_hbm, class_hbm, slots_hbm, mix_hbm, metric_hbm, nb_hbm, dx_hbm, dy_hbm,
                   send_hbm, tend_ref, m_ref, mine_a_ref, mine_b_ref, out_ref, in_ref, mrow_ref,
                   k32, kk, state_ref, class_ref, slot_ref, mix_ref, x0, yy, tt, rr, qa, qb, send_ref,
                   metric_ref, nb_ref, dx_ref, dy_ref, dxs, dys, fcm_ref, sems):
    me = me_ref[0]
    load_slots = pltpu.make_async_copy(
        slots_hbm.at[:, pl.ds(pl.multiple_of(me // 4 * 128, 128), 128)], slot_ref, sems.at[0])
    load_state = pltpu.make_async_copy(state_hbm, state_ref, sems.at[1])
    load_class = pltpu.make_async_copy(class_hbm, class_ref, sems.at[2])
    load_mix = pltpu.make_async_copy(mix_hbm, mix_ref, sems.at[3])
    load_fcm = pltpu.make_async_copy(fcm_hbm, fcm_ref, sems.at[4])
    load_metric = pltpu.make_async_copy(metric_hbm, metric_ref, sems.at[5])
    load_nb = pltpu.make_async_copy(nb_hbm, nb_ref, sems.at[6])
    load_dx = pltpu.make_async_copy(dx_hbm, dx_ref, sems.at[7])
    load_dy = pltpu.make_async_copy(dy_hbm, dy_ref, sems.at[8])
    load_fcm.start()
    load_mix.start()
    load_slots.start()
    load_class.start()
    load_state.start()
    load_nb.start()
    load_metric.start()
    load_dx.start()
    load_dy.start()
    for load in (load_fcm, load_mix, load_slots, load_class, load_nb, load_metric, load_dx, load_dy, load_state):
        load.wait()
    tables(me * MEMBERS, nb_ref, metric_ref, out_ref, in_ref, mrow_ref)
    rep = jnp.where(
        (iota((LEVELS, WIDE), 1) % LEVELS == iota((LEVELS, WIDE), 0)) & (iota((LEVELS, WIDE), 1) < ROWS), 1.0, 0.0
    ).astype(BF16)
    lane = iota((1, WIDE), 1)
    for f in range(FIELDS):
        crow = jnp.zeros((1, WIDE), F32)
        for g in range(FIELDS):
            crow = jnp.where((lane >= LEVELS * g) & (lane < LEVELS * g + LEVELS), PHYSICS_RATE * fcm_ref[g, f], crow)
        mh, ml = split2(jnp.transpose(mix_ref[f]))
        k32[LEVELS * f:LEVELS * f + LEVELS, :] = (dot(mh, rep) + dot(ml, rep)) * crow
    k32[ROWS:WIDE, :] = jnp.zeros((WIDE - ROWS, WIDE), F32)
    hi, lo = split2(k32[...])
    kk[0:WIDE, :] = hi
    kk[WIDE:, :] = lo
    part = me % 4
    own = slot_ref[:, 0:MEMBERS]
    for j in range(1, 4):
        own = jnp.where(part == j, slot_ref[:, MEMBERS * j:MEMBERS * j + MEMBERS], own)
    cls = expand_points(class_ref[...].astype(F32))
    slot = expand_points(own.astype(F32))
    col = iota((1, COLS), 1).astype(F32)
    crank = rank_row((4.0 - cls) * COLS + col)
    srank = rank_row(slot)
    place = slot - jnp.floor(slot * (1.0 / COLS)) * COLS
    perm = jnp.where(iota((COLS, COLS), 0).astype(F32) == crank, 1.0, 0.0).astype(BF16)
    extra = jnp.where(iota((128, COLS), 0) == 0, place, 0.0)
    eh, el = split2(extra)
    x0[:, ROWS:WIDE] = (dot_nt(perm, eh) + dot_nt(perm, el))[:, 0:WIDE - ROWS]
    rh, rl = split2(jnp.broadcast_to(srank, (16, COLS)))
    srank_sorted = (dot_nt(rh, perm) + dot_nt(rl, perm))[0:1, :]
    n1 = jnp.sum(jnp.where(cls > 1.5, 1, 0))
    n2 = jnp.sum(jnp.where(cls > 2.5, 1, 0))
    n3 = jnp.sum(jnp.where(cls > 3.5, 1, 0))
    sh, sl = split2(state_ref[...])
    x0[:, 0:ROWS] = dot_nt(perm, sh) + dot_nt(perm, sl)
    rates(state_ref[...], dx_ref, dy_ref, dxs, dys)
    xh, xl = split2(x0[...])
    xhh = jnp.concatenate([xh, xh], axis=1)
    for n in range(0, WIDE, 256):
        at = slice(n, n + 256)
        y = (dot(xl, kk[0:WIDE, at]) + dot(xhh, kk[:, at])) * (1.0 / PHYSICS_RATE)
        yy[:, at] = y
        t = jnp.tanh(y)
        tt[:, at] = t
        q = t.astype(BF16)
        rr[:, at] = t - q.astype(F32)
        qa[:, at] = q

    def step(rows, live, old, new, low):
        deep = 2 * WIDE if low else WIDE
        acc = dot(old[0:rows, 0:deep], kk[0:deep, :])
        for b in range(0, rows, 32):
            rb = slice(b, b + 32)
            y = yy[rb, :] + acc[rb]
            yy[rb, :] = y
            t = jnp.tanh(y)
            if b + 32 > max((0,) + tuple(n for n in SIZES if n < rows)):
                tt[rb, :] += jnp.where(iota((32, WIDE), 0) + b < live, t, 0.0)
            else:
                tt[rb, :] += t
            s = t + rr[rb, :]
            q = s.astype(BF16)
            rr[rb, :] = s - q.astype(F32)
            new[rb, 0:WIDE] = q
            if not low:
                new[rb, WIDE:] = (old[rb, 0:WIDE].astype(F32) + q.astype(F32)).astype(BF16)

    def sweep(k, old, new, low):
        live = jnp.where(k < 4, COLS, jnp.where(k < 8, n1, jnp.where(k < 12, n2, jnp.where(k < 16, n3, 0))))
        for below, rows in zip((0,) + SIZES, SIZES):
            @pl.when((live > below) & (live <= rows))
            def _():
                step(rows, live, old, new, low)

    def two_sweeps(j, _):
        sweep(2 * j + 1, qa, qb, False)
        sweep(2 * j + 2, qb, qa, True)
        return 0

    lax.fori_loop(0, 8, two_sweeps, 0)
    q_send = jnp.where(iota((COLS, COLS), 0).astype(F32) == srank_sorted, 1.0, 0.0).astype(BF16)
    fh, fl = split2(x0[...] + PHYSICS_RATE * tt[...])
    out = dot(q_send, fh) + dot(q_send, fl)
    send_ref[...] = out.reshape(COLS // 4, 4, WIDE)
    store_send = pltpu.make_async_copy(send_ref, send_hbm, sems.at[9])
    store_send.start()
    th, tl = split2(jnp.transpose(tt[...])[0:ROWS, :] * (PHYSICS_RATE / SUBSTEPS))
    tend_ref[...] = dot(th, perm) + dot(tl, perm)
    move(lambda at, n: state_ref[pl.ds(at, n), :], tend_ref, mrow_ref, out_ref, dxs, dys, m_ref, mine_a_ref, mine_b_ref)
    store_send.wait()


HALO = ((MEMBERS, WIDE), F32)
MOVED = ((TALL, COLS), F32)
GRID = ((ROWS, COLS), F32)


def physics_call(state2, cost_class, batch_slot, level_mix, fcm, me, metric, neighbours, dx, dy):
    work = [((WIDE, WIDE), F32), ((2 * WIDE, WIDE), BF16), GRID, ((16, MEMBERS), jnp.int32),
            ((16, 128), jnp.int32), ((FIELDS, LEVELS, LEVELS), F32)]
    work += [((COLS, WIDE), F32)] * 4 + [((COLS, WIDE), BF16), ((COLS, 2 * WIDE), BF16), ((COLS // 4, 4, WIDE), F32)]
    work += [((16, MEMBERS), F32), ((4, MEMBERS), jnp.int32), ((256, 256), F32), ((256, 256), F32), GRID, GRID]
    out = [((COLS // 4, 4, WIDE), F32), GRID, MOVED, HALO, HALO, ((2 * MEMBERS, COLS), BF16),
           ((2 * MEMBERS, COLS), BF16), ((8, COLS), F32)]
    shapes = tuple((pltpu.HBM if k < 1 else pltpu.VMEM)(s, t) for k, (s, t) in enumerate(out))
    return pl.pallas_call(
        physics_kernel, out_shape=shapes, in_specs=[SM] + [HB] * 9, out_specs=(HB,) + (VM,) * 7,
        scratch_shapes=[pltpu.VMEM(s, t) for s, t in work]
        + [pltpu.SMEM((FIELDS, FIELDS), F32), pltpu.SemaphoreType.DMA((10,))],
        compiler_params=PARAMS, name="physics",
    )(me, *in_hbm(fcm, state2, cost_class, batch_slot, level_mix, metric, neighbours, dx, dy))


def element_tables(neighbours_ref, base):
    local = neighbours_ref[...] - base
    outside = (local < 0) | (local >= MEMBERS)
    wide = jnp.concatenate([local.astype(F32), jnp.where(outside, 1.0, 0.0)], axis=0)
    spread = jnp.where(iota((MEMBERS, COLS), 1) // 16 == iota((MEMBERS, COLS), 0), 1.0, 0.0)
    by_column = jnp.dot(wide, spread, precision=HIGHEST, preferred_element_type=F32)
    return wide, by_column, spread


def east_west(by_column):
    col = iota((1, COLS), 1)
    ix, line = col % 4, (col % 16) // 4 * 4
    source = jnp.where(ix == 3, 16.0 * by_column[0:1] + line.astype(F32),
                       jnp.where(ix == 0, 16.0 * by_column[1:2] + (line + 3).astype(F32), -1.0))
    row = iota((COLS, COLS), 0)
    hit = (row.astype(F32) == source) | (row == iota((COLS, COLS), 1))
    return jnp.where(hit, 1.0, 0.0).astype(BF16)


def north_south(by_column):
    col = iota((1, COLS), 1)
    ix, iy = (col % 4).astype(F32), (col % 16) // 4
    north = jnp.where(by_column[6:7] > 0.5, -1.0, 16.0 * by_column[2:3] + ix)
    south = jnp.where(by_column[7:8] > 0.5, -1.0, 16.0 * by_column[3:4] + 12.0 + ix)
    source = jnp.where(iy == 3, north, jnp.where(iy == 0, south, -1.0))
    row = iota((COLS, COLS), 0)
    hit = (row.astype(F32) == source) | (row == iota((COLS, COLS), 1))
    return jnp.where(hit, 1.0, 0.0).astype(BF16)


def rank_among(key, member, spread):
    key8 = jnp.broadcast_to(jnp.where(member > 0.5, key, 1e9), (8, MEMBERS))
    key_col = jnp.transpose(key8)[:, 0:1]
    rank = jnp.sum(jnp.where(key_col < key, 1.0, 0.0), axis=0, keepdims=True)
    return jnp.dot(jnp.broadcast_to(rank, (8, MEMBERS)), spread, precision=HIGHEST,
                   preferred_element_type=F32)[0:1]


def halo_targets(wide, by_column, spread):
    col = iota((1, COLS), 1)
    ix, iy = (col % 4).astype(F32), (col % 16) // 4
    own = iota((1, MEMBERS), 1).astype(F32)
    up, down = by_column[6:7] > 0.5, by_column[7:8] > 0.5
    to_north = jnp.where((iy == 3) & up, 8.0 * ix + rank_among(own, wide[6:7], spread), -1.0)
    to_south = jnp.where((iy == 0) & down, 8.0 * ix + rank_among(own, wide[7:8], spread), -1.0)
    from_south = jnp.where((iy == 0) & down, 8.0 * ix + rank_among(wide[3:4], wide[7:8], spread), -1.0)
    from_north = jnp.where((iy == 3) & up, 8.0 * ix + rank_among(wide[2:3], wide[6:7], spread), -1.0)
    return to_north, to_south, from_south, from_north


def two_selections(first, second):
    row = iota((2 * MEMBERS, COLS), 0).astype(F32)
    hit = (row == first) | ((row - MEMBERS == second) & (second > -0.5))
    return jnp.where(hit, 1.0, 0.0).astype(BF16)


def whole_kernel(base_ref, neighbours_ref, whole_ref):
    base = base_ref[0]
    _, by_column, _ = element_tables(neighbours_ref, base)
    whole_ref[...] = dot(east_west(by_column), north_south(by_column)).astype(BF16)


def tables(base, neighbours_ref, metric_ref, out_ref, in_ref, mrow_ref):
    wide, by_column, spread = element_tables(neighbours_ref, base)
    to_north, to_south, from_south, from_north = halo_targets(wide, by_column, spread)
    odd = base // MEMBERS % 2 == 1
    sent = two_selections(jnp.where(odd, to_south, to_north), jnp.where(odd, to_north, to_south))
    out_ref[...] = dot_nt(sent, east_west(by_column)).astype(BF16)
    in_ref[...] = two_selections(jnp.where(odd, from_south, from_north), jnp.where(odd, from_north, from_south))
    mrow_ref[...] = jnp.broadcast_to(expand_points(metric_ref[...]), (8, COLS))


def rates(value, dx_ref, dy_ref, dxs, dys):
    vh, vl = split2(value)
    for half in (0, 256):
        at = slice(half, half + 256)
        for d_ref, acc in ((dx_ref, dxs), (dy_ref, dys)):
            dh, dl = split2(d_ref[...])
            acc[:, at] = dot(vh[:, at], dh) + dot(vl[:, at], dh) + dot(vh[:, at], dl)


def move(read, tend_ref, mrow_ref, out_ref, dxs, dys, m_ref, mine_a_ref, mine_b_ref):
    metric = mrow_ref[0:1, :]
    u, v = read(0, LEVELS), read(LEVELS, LEVELS)
    for f in range(FIELDS):
        at = pl.ds(LEVELS * f, LEVELS)
        rate = u * dxs[at, :] + v * dys[at, :]
        m_ref[at, :] = metric * ((read(LEVELS * f, LEVELS) - TIME_STEP * rate) + tend_ref[at, :])
    m_ref[ROWS:TALL, :] = mrow_ref[...]
    mh, ml = split2(m_ref[...])
    halo = dot_nt(out_ref[...], mh) + dot_nt(out_ref[...], ml)
    mine_a_ref[:, 0:TALL] = halo[0:MEMBERS]
    mine_b_ref[:, 0:TALL] = halo[MEMBERS:]
    mine_a_ref[:, TALL:WIDE] = jnp.zeros((MEMBERS, WIDE - TALL), F32)
    mine_b_ref[:, TALL:WIDE] = jnp.zeros((MEMBERS, WIDE - TALL), F32)


def sum_kernel(m_ref, whole_ref, l_ref):
    mh, ml = split2(m_ref[...])
    l_ref[...] = dot(mh, whole_ref[...]) + dot(ml, whole_ref[...])


def finish(l_ref, prev_ref, next_ref, in_ref, c_ref, done=lambda at: None):
    halo = jnp.concatenate([prev_ref[...], next_ref[...]], axis=0)
    hh, hl = split2(jnp.transpose(halo)[0:TALL, :])
    mass = l_ref[ROWS:TALL, :] + dot(hh[ROWS:TALL], in_ref[...]) + dot(hl[ROWS:TALL], in_ref[...])
    inverse = 1.0 / mass[0:1, :]
    for at in CHUNKS:
        c_ref[at, :] = (l_ref[at, :] + dot(hh[at], in_ref[...]) + dot(hl[at], in_ref[...])) * inverse
        done(at)


CHUNKS = tuple(slice(a, a + 144) for a in range(0, ROWS, 144))


def storing(body, source, target, sems):
    copies = []

    def done(at):
        copies.append(pltpu.make_async_copy(source.at[at], target.at[at], sems.at[len(copies)]))
        copies[-1].start()

    body(done)
    for copy in copies:
        copy.wait()


def finish_kernel(l_ref, prev_ref, next_ref, in_ref, out_hbm, cur, sems):
    storing(lambda done: finish(l_ref, prev_ref, next_ref, in_ref, cur, done), cur, out_hbm, sems)


def next_kernel(l_ref, prev_ref, next_ref, in_ref, tend_ref, mrow_ref, dx_ref, dy_ref, out_ref,
                m_ref, mine_a_ref, mine_b_ref, cur, dxs, dys):
    finish(l_ref, prev_ref, next_ref, in_ref, cur)
    rates(cur[...], dx_ref, dy_ref, dxs, dys)
    move(lambda at, n: cur[pl.ds(at, n), :], tend_ref, mrow_ref, out_ref, dxs, dys, m_ref, mine_a_ref, mine_b_ref)


def place_kernel(arrived_hbm, out_hbm, arrived_ref, cur, sems):
    pltpu.sync_copy(arrived_hbm, arrived_ref)
    rows = arrived_ref[...].reshape(COLS, WIDE)
    place_col = rows[:, ROWS:ROWS + 1]
    pick = jnp.where(iota((COLS, COLS), 1).astype(F32) == place_col, 1.0, 0.0).astype(BF16)
    hi, lo = split2(jnp.transpose(rows)[0:ROWS, :])

    def body(done):
        for at in CHUNKS:
            cur[at, :] = dot(hi[at], pick) + dot(lo[at], pick)
            done(at)

    storing(body, cur, out_hbm, sems)


def call(kernel, out, specs, scratch=(), semaphores=0, hbm_out=0):
    shapes = tuple((pltpu.HBM if k < hbm_out else pltpu.VMEM)(s, t) for k, (s, t) in enumerate(out))
    work = [pltpu.VMEM(s, t) for s, t in scratch]
    if semaphores:
        work.append(pltpu.SemaphoreType.DMA((semaphores,)))
    return pl.pallas_call(
        kernel, out_shape=shapes, in_specs=specs, out_specs=(HB,) * hbm_out + (VM,) * (len(out) - hbm_out),
        scratch_shapes=work, compiler_params=PARAMS)


def in_hbm(*arrays):
    return tuple(pltpu.with_memory_space_constraint(a, pltpu.HBM) for a in arrays)


def swapped(array, first):
    length = lax.axis_size(AXES)
    low = range(0 if first else 1, length, 2)
    pairs = [(i, (i + 1) % length) for i in low]
    return lax.ppermute(array, AXES, pairs + [(j, i) for i, j in pairs])


def step(state, metric, neighbours, cost_class, batch_slot, level_mix, field_coupling_matrix):
    me = lax.axis_index(AXES).astype(jnp.int32).reshape(1)
    base = me * MEMBERS
    state2 = state.reshape(ROWS, COLS)
    dx, dy = (jnp.asarray(a) for a in derivative_blocks())
    send, tend, m, mine_a, mine_b, out_rows, in_rows, mrow = physics_call(
        state2, cost_class, batch_slot, level_mix, field_coupling_matrix, me, metric, neighbours, dx, dy)
    (whole,) = call(whole_kernel, [((COLS, COLS), BF16)], [SM, VM])(base, neighbours)
    arrived = lax.all_to_all(send, AXES, split_axis=0, concat_axis=0, tiled=True)
    for substep in range(SUBSTEPS):
        theirs_b = swapped(mine_b, False)
        theirs_a = swapped(mine_a, True)
        (total,) = call(sum_kernel, [MOVED], [VM, VM])(m, whole)
        if substep < SUBSTEPS - 1:
            m, mine_a, mine_b = call(next_kernel, [MOVED, HALO, HALO], [VM] * 9, [GRID] * 3)(
                total, theirs_a, theirs_b, in_rows, tend, mrow, dx, dy, out_rows)
    (physics_state,) = call(place_kernel, [GRID], [HB], [((COLS // 4, 4, WIDE), F32), GRID], len(CHUNKS), 1)(
        *in_hbm(arrived))
    (state_out,) = call(finish_kernel, [GRID], [VM] * 4, [GRID], len(CHUNKS), 1)(
        total, theirs_a, theirs_b, in_rows)
    return state_out.reshape(state.shape), physics_state.reshape(state.shape)


def solution(mesh):
    split = P(None, AXES)
    whole = P(None, None, AXES)
    return jax.shard_map(
        step, mesh=mesh, in_specs=(whole, split, split, split, P(), P(), P()),
        out_specs=(whole, whole), check_vma=False)
```

```python
import jax
import jax.numpy as jnp
import numpy as np
from jax import lax
from jax.experimental import pallas as pl
from jax.experimental.pallas import tpu as pltpu
from jax.sharding import PartitionSpec as P


AXES = ("elem", "face")
F32 = jnp.float32
BF16 = jnp.bfloat16
HIGHEST = lax.Precision.HIGHEST
FIELDS, LEVELS, SUBSTEPS = 10, 72, 3
ROWS, COLS, MEMBERS, WIDE = 720, 512, 32, 768
TALL = ROWS + 8
PHYSICS_RATE, TIME_STEP = 0.1, 0.02
VM = pl.BlockSpec(memory_space=pltpu.VMEM)
HB = pl.BlockSpec(memory_space=pltpu.HBM)
SM = pl.BlockSpec(memory_space=pltpu.SMEM)
PARAMS = pltpu.CompilerParams(vmem_limit_bytes=30 << 20)


def gll_matrix():
    nodes = np.array([-1.0, -1.0 / np.sqrt(5.0), 1.0 / np.sqrt(5.0), 1.0])
    derivative = np.zeros((4, 4))
    for i in range(4):
        for j in range(4):
            others = [k for k in range(4) if k != j]
            if i == j:
                derivative[i, j] = sum(1.0 / (nodes[j] - nodes[k]) for k in others)
            else:
                top = np.prod([nodes[i] - nodes[k] for k in others if k != i])
                derivative[i, j] = top / np.prod([nodes[j] - nodes[k] for k in others])
    return derivative


def derivative_blocks():
    d = gll_matrix()
    across = np.kron(np.eye(4), d).astype(np.float32).T
    upward = np.kron(d, np.eye(4)).astype(np.float32).T
    return np.kron(np.eye(16), across).astype(np.float32), np.kron(np.eye(16), upward).astype(np.float32)


SIZES = (160, 288, 416, COLS)


def split2(v):
    hi = v.astype(BF16)
    return hi, (v - hi.astype(F32)).astype(BF16)


def dot(a, b):
    return jnp.dot(a, b, preferred_element_type=F32)


def dot_nt(a, b):
    return lax.dot_general(a, b, (((1,), (1,)), ((), ())), preferred_element_type=F32)


def iota(shape, dim):
    return lax.broadcasted_iota(jnp.int32, shape, dim)


def expand_points(table):
    spread = jnp.where(iota((32, COLS), 1) // 16 == iota((32, COLS), 0), 1.0, 0.0)
    wide = jnp.dot(table, spread, precision=HIGHEST, preferred_element_type=F32)
    wide = jnp.where(iota((16, COLS), 1) % 16 == iota((16, COLS), 0), wide, 0.0)
    return jnp.sum(wide, axis=0, keepdims=True)


def as_column(row):
    return jnp.transpose(jnp.broadcast_to(row, (8, COLS)))[:, 0:1]


def rank_row(key_row):
    key_col = as_column(key_row)
    return jnp.sum(jnp.where(key_col < key_row, 1.0, 0.0), axis=0, keepdims=True)


def physics_kernel(me_ref, fcm_hbm, state_hbm, class_hbm, slots_hbm, mix_hbm, metric_hbm, nb_hbm, dx_hbm, dy_hbm,
                   send_hbm, tend_ref, m_ref, mine_a_ref, mine_b_ref, out_ref, in_ref, mrow_ref,
                   k32, kk, state_ref, class_ref, slot_ref, mix_ref, x0, yy, tt, rr, qa, qb, send_ref,
                   metric_ref, nb_ref, dx_ref, dy_ref, dxs, dys, fcm_ref, sems):
    me = me_ref[0]
    load_slots = pltpu.make_async_copy(
        slots_hbm.at[:, pl.ds(pl.multiple_of(me // 4 * 128, 128), 128)], slot_ref, sems.at[0])
    load_state = pltpu.make_async_copy(state_hbm, state_ref, sems.at[1])
    load_class = pltpu.make_async_copy(class_hbm, class_ref, sems.at[2])
    load_mix = pltpu.make_async_copy(mix_hbm, mix_ref, sems.at[3])
    load_fcm = pltpu.make_async_copy(fcm_hbm, fcm_ref, sems.at[4])
    load_metric = pltpu.make_async_copy(metric_hbm, metric_ref, sems.at[5])
    load_nb = pltpu.make_async_copy(nb_hbm, nb_ref, sems.at[6])
    load_dx = pltpu.make_async_copy(dx_hbm, dx_ref, sems.at[7])
    load_dy = pltpu.make_async_copy(dy_hbm, dy_ref, sems.at[8])
    load_fcm.start()
    load_mix.start()
    load_slots.start()
    load_class.start()
    load_state.start()
    load_nb.start()
    load_metric.start()
    load_dx.start()
    load_dy.start()
    for load in (load_fcm, load_mix, load_slots, load_class, load_nb, load_metric, load_dx, load_dy, load_state):
        load.wait()
    tables(me * MEMBERS, nb_ref, metric_ref, out_ref, in_ref, mrow_ref)
    rep = jnp.where(
        (iota((LEVELS, WIDE), 1) % LEVELS == iota((LEVELS, WIDE), 0)) & (iota((LEVELS, WIDE), 1) < ROWS), 1.0, 0.0
    ).astype(BF16)
    lane = iota((1, WIDE), 1)
    for f in range(FIELDS):
        crow = jnp.zeros((1, WIDE), F32)
        for g in range(FIELDS):
            crow = jnp.where((lane >= LEVELS * g) & (lane < LEVELS * g + LEVELS), PHYSICS_RATE * fcm_ref[g, f], crow)
        mh, ml = split2(jnp.transpose(mix_ref[f]))
        k32[LEVELS * f:LEVELS * f + LEVELS, :] = (dot(mh, rep) + dot(ml, rep)) * crow
    k32[ROWS:WIDE, :] = jnp.zeros((WIDE - ROWS, WIDE), F32)
    hi, lo = split2(k32[...])
    kk[0:WIDE, :] = hi
    kk[WIDE:, :] = lo
    part = me % 4
    own = slot_ref[:, 0:MEMBERS]
    for j in range(1, 4):
        own = jnp.where(part == j, slot_ref[:, MEMBERS * j:MEMBERS * j + MEMBERS], own)
    cls = expand_points(class_ref[...].astype(F32))
    slot = expand_points(own.astype(F32))
    col = iota((1, COLS), 1).astype(F32)
    crank = rank_row((4.0 - cls) * COLS + col)
    srank = rank_row(slot)
    place = slot - jnp.floor(slot * (1.0 / COLS)) * COLS
    perm = jnp.where(iota((COLS, COLS), 0).astype(F32) == crank, 1.0, 0.0).astype(BF16)
    extra = jnp.where(iota((128, COLS), 0) == 0, place, 0.0)
    eh, el = split2(extra)
    x0[:, ROWS:WIDE] = (dot_nt(perm, eh) + dot_nt(perm, el))[:, 0:WIDE - ROWS]
    rh, rl = split2(jnp.broadcast_to(srank, (16, COLS)))
    srank_sorted = (dot_nt(rh, perm) + dot_nt(rl, perm))[0:1, :]
    n1 = jnp.sum(jnp.where(cls > 1.5, 1, 0))
    n2 = jnp.sum(jnp.where(cls > 2.5, 1, 0))
    n3 = jnp.sum(jnp.where(cls > 3.5, 1, 0))
    sh, sl = split2(state_ref[...])
    x0[:, 0:ROWS] = dot_nt(perm, sh) + dot_nt(perm, sl)
    rates(state_ref[...], dx_ref, dy_ref, dxs, dys)
    xh, xl = split2(x0[...])
    xhh = jnp.concatenate([xh, xh], axis=1)
    for n in range(0, WIDE, 256):
        at = slice(n, n + 256)
        y = (dot(xl, kk[0:WIDE, at]) + dot(xhh, kk[:, at])) * (1.0 / PHYSICS_RATE)
        yy[:, at] = y
        t = jnp.tanh(y)
        tt[:, at] = t
        q = t.astype(BF16)
        rr[:, at] = t - q.astype(F32)
        qa[:, at] = q

    def step(rows, live, old, new, low):
        deep = 2 * WIDE if low else WIDE
        acc = dot(old[0:rows, 0:deep], kk[0:deep, :])
        for b in range(0, rows, 32):
            rb = slice(b, b + 32)
            y = yy[rb, :] + acc[rb]
            yy[rb, :] = y
            t = jnp.tanh(y)
            if b + 32 > max((0,) + tuple(n for n in SIZES if n < rows)):
                tt[rb, :] += jnp.where(iota((32, WIDE), 0) + b < live, t, 0.0)
            else:
                tt[rb, :] += t
            s = t + rr[rb, :]
            q = s.astype(BF16)
            rr[rb, :] = s - q.astype(F32)
            new[rb, 0:WIDE] = q
            if not low:
                new[rb, WIDE:] = (old[rb, 0:WIDE].astype(F32) + q.astype(F32)).astype(BF16)

    def sweep(k, old, new, low):
        live = jnp.where(k < 4, COLS, jnp.where(k < 8, n1, jnp.where(k < 12, n2, jnp.where(k < 16, n3, 0))))
        for below, rows in zip((0,) + SIZES, SIZES):
            @pl.when((live > below) & (live <= rows))
            def _():
                step(rows, live, old, new, low)

    def two_sweeps(j, _):
        sweep(2 * j + 1, qa, qb, False)
        sweep(2 * j + 2, qb, qa, True)
        return 0

    lax.fori_loop(0, 8, two_sweeps, 0)
    q_send = jnp.where(iota((COLS, COLS), 0).astype(F32) == srank_sorted, 1.0, 0.0).astype(BF16)
    fh, fl = split2(x0[...] + PHYSICS_RATE * tt[...])
    out = dot(q_send, fh) + dot(q_send, fl)
    send_ref[...] = out.reshape(COLS // 4, 4, WIDE)
    store_send = pltpu.make_async_copy(send_ref, send_hbm, sems.at[9])
    store_send.start()
    th, tl = split2(jnp.transpose(tt[...])[0:ROWS, :] * (PHYSICS_RATE / SUBSTEPS))
    tend_ref[...] = dot(th, perm) + dot(tl, perm)
    move(lambda at, n: state_ref[pl.ds(at, n), :], tend_ref, mrow_ref, out_ref, dxs, dys, m_ref, mine_a_ref, mine_b_ref)
    store_send.wait()


HALO = ((MEMBERS, WIDE), F32)
MOVED = ((TALL, COLS), F32)
GRID = ((ROWS, COLS), F32)


def physics_call(state2, cost_class, batch_slot, level_mix, fcm, me, metric, neighbours, dx, dy):
    work = [((WIDE, WIDE), F32), ((2 * WIDE, WIDE), BF16), GRID, ((16, MEMBERS), jnp.int32),
            ((16, 128), jnp.int32), ((FIELDS, LEVELS, LEVELS), F32)]
    work += [((COLS, WIDE), F32)] * 4 + [((COLS, WIDE), BF16), ((COLS, 2 * WIDE), BF16), ((COLS // 4, 4, WIDE), F32)]
    work += [((16, MEMBERS), F32), ((4, MEMBERS), jnp.int32), ((256, 256), F32), ((256, 256), F32), GRID, GRID]
    out = [((COLS // 4, 4, WIDE), F32), GRID, MOVED, HALO, HALO, ((2 * MEMBERS, COLS), BF16),
           ((2 * MEMBERS, COLS), BF16), ((8, COLS), F32)]
    shapes = tuple((pltpu.HBM if k < 1 else pltpu.VMEM)(s, t) for k, (s, t) in enumerate(out))
    return pl.pallas_call(
        physics_kernel, out_shape=shapes, in_specs=[SM] + [HB] * 9, out_specs=(HB,) + (VM,) * 7,
        scratch_shapes=[pltpu.VMEM(s, t) for s, t in work]
        + [pltpu.SMEM((FIELDS, FIELDS), F32), pltpu.SemaphoreType.DMA((10,))],
        compiler_params=PARAMS, name="physics",
    )(me, *in_hbm(fcm, state2, cost_class, batch_slot, level_mix, metric, neighbours, dx, dy))


def element_tables(neighbours_ref, base):
    local = neighbours_ref[...] - base
    outside = (local < 0) | (local >= MEMBERS)
    wide = jnp.concatenate([local.astype(F32), jnp.where(outside, 1.0, 0.0)], axis=0)
    spread = jnp.where(iota((MEMBERS, COLS), 1) // 16 == iota((MEMBERS, COLS), 0), 1.0, 0.0)
    by_column = jnp.dot(wide, spread, precision=HIGHEST, preferred_element_type=F32)
    return wide, by_column, spread


def east_west(by_column):
    col = iota((1, COLS), 1)
    ix, line = col % 4, (col % 16) // 4 * 4
    source = jnp.where(ix == 3, 16.0 * by_column[0:1] + line.astype(F32),
                       jnp.where(ix == 0, 16.0 * by_column[1:2] + (line + 3).astype(F32), -1.0))
    row = iota((COLS, COLS), 0)
    hit = (row.astype(F32) == source) | (row == iota((COLS, COLS), 1))
    return jnp.where(hit, 1.0, 0.0).astype(BF16)


def north_south(by_column):
    col = iota((1, COLS), 1)
    ix, iy = (col % 4).astype(F32), (col % 16) // 4
    north = jnp.where(by_column[6:7] > 0.5, -1.0, 16.0 * by_column[2:3] + ix)
    south = jnp.where(by_column[7:8] > 0.5, -1.0, 16.0 * by_column[3:4] + 12.0 + ix)
    source = jnp.where(iy == 3, north, jnp.where(iy == 0, south, -1.0))
    row = iota((COLS, COLS), 0)
    hit = (row.astype(F32) == source) | (row == iota((COLS, COLS), 1))
    return jnp.where(hit, 1.0, 0.0).astype(BF16)


def rank_among(key, member, spread):
    key8 = jnp.broadcast_to(jnp.where(member > 0.5, key, 1e9), (8, MEMBERS))
    key_col = jnp.transpose(key8)[:, 0:1]
    rank = jnp.sum(jnp.where(key_col < key, 1.0, 0.0), axis=0, keepdims=True)
    return jnp.dot(jnp.broadcast_to(rank, (8, MEMBERS)), spread, precision=HIGHEST,
                   preferred_element_type=F32)[0:1]


def halo_targets(wide, by_column, spread):
    col = iota((1, COLS), 1)
    ix, iy = (col % 4).astype(F32), (col % 16) // 4
    own = iota((1, MEMBERS), 1).astype(F32)
    up, down = by_column[6:7] > 0.5, by_column[7:8] > 0.5
    to_north = jnp.where((iy == 3) & up, 8.0 * ix + rank_among(own, wide[6:7], spread), -1.0)
    to_south = jnp.where((iy == 0) & down, 8.0 * ix + rank_among(own, wide[7:8], spread), -1.0)
    from_south = jnp.where((iy == 0) & down, 8.0 * ix + rank_among(wide[3:4], wide[7:8], spread), -1.0)
    from_north = jnp.where((iy == 3) & up, 8.0 * ix + rank_among(wide[2:3], wide[6:7], spread), -1.0)
    return to_north, to_south, from_south, from_north


def two_selections(first, second):
    row = iota((2 * MEMBERS, COLS), 0).astype(F32)
    hit = (row == first) | ((row - MEMBERS == second) & (second > -0.5))
    return jnp.where(hit, 1.0, 0.0).astype(BF16)


def whole_kernel(base_ref, neighbours_ref, whole_ref):
    base = base_ref[0]
    _, by_column, _ = element_tables(neighbours_ref, base)
    whole_ref[...] = dot(east_west(by_column), north_south(by_column)).astype(BF16)


def tables(base, neighbours_ref, metric_ref, out_ref, in_ref, mrow_ref):
    wide, by_column, spread = element_tables(neighbours_ref, base)
    to_north, to_south, from_south, from_north = halo_targets(wide, by_column, spread)
    odd = base // MEMBERS % 2 == 1
    sent = two_selections(jnp.where(odd, to_south, to_north), jnp.where(odd, to_north, to_south))
    out_ref[...] = dot_nt(sent, east_west(by_column)).astype(BF16)
    in_ref[...] = two_selections(jnp.where(odd, from_south, from_north), jnp.where(odd, from_north, from_south))
    mrow_ref[...] = jnp.broadcast_to(expand_points(metric_ref[...]), (8, COLS))


def rates(value, dx_ref, dy_ref, dxs, dys):
    vh, vl = split2(value)
    for half in (0, 256):
        at = slice(half, half + 256)
        for d_ref, acc in ((dx_ref, dxs), (dy_ref, dys)):
            dh, dl = split2(d_ref[...])
            acc[:, at] = dot(vh[:, at], dh) + dot(vl[:, at], dh) + dot(vh[:, at], dl)


def move(read, tend_ref, mrow_ref, out_ref, dxs, dys, m_ref, mine_a_ref, mine_b_ref):
    metric = mrow_ref[0:1, :]
    u, v = read(0, LEVELS), read(LEVELS, LEVELS)
    for f in range(FIELDS):
        at = pl.ds(LEVELS * f, LEVELS)
        rate = u * dxs[at, :] + v * dys[at, :]
        m_ref[at, :] = metric * ((read(LEVELS * f, LEVELS) - TIME_STEP * rate) + tend_ref[at, :])
    m_ref[ROWS:TALL, :] = mrow_ref[...]
    mh, ml = split2(m_ref[...])
    halo = dot_nt(out_ref[...], mh) + dot_nt(out_ref[...], ml)
    mine_a_ref[:, 0:TALL] = halo[0:MEMBERS]
    mine_b_ref[:, 0:TALL] = halo[MEMBERS:]
    mine_a_ref[:, TALL:WIDE] = jnp.zeros((MEMBERS, WIDE - TALL), F32)
    mine_b_ref[:, TALL:WIDE] = jnp.zeros((MEMBERS, WIDE - TALL), F32)


def sum_kernel(m_ref, whole_ref, l_ref):
    mh, ml = split2(m_ref[...])
    l_ref[...] = dot(mh, whole_ref[...]) + dot(ml, whole_ref[...])


def finish(l_ref, prev_ref, next_ref, in_ref, c_ref, done=lambda at: None):
    halo = jnp.concatenate([prev_ref[...], next_ref[...]], axis=0)
    both = jnp.concatenate(split2(jnp.transpose(halo)[0:TALL, :]), axis=1)
    places = jnp.concatenate([in_ref[...], in_ref[...]], axis=0)
    mass = l_ref[ROWS:TALL, :] + dot(both[ROWS:TALL], places)
    inverse = 1.0 / mass[0:1, :]
    for at in CHUNKS:
        c_ref[at, :] = (l_ref[at, :] + dot(both[at], places)) * inverse
        done(at)


CHUNKS = tuple(slice(a, a + 144) for a in range(0, ROWS, 144))


def storing(body, source, target, sems):
    copies = []

    def done(at):
        copies.append(pltpu.make_async_copy(source.at[at], target.at[at], sems.at[len(copies)]))
        copies[-1].start()

    body(done)
    for copy in copies:
        copy.wait()


def finish_kernel(l_ref, prev_ref, next_ref, in_ref, out_hbm, cur, sems):
    storing(lambda done: finish(l_ref, prev_ref, next_ref, in_ref, cur, done), cur, out_hbm, sems)


def next_kernel(l_ref, prev_ref, next_ref, in_ref, tend_ref, mrow_ref, dx_ref, dy_ref, out_ref,
                m_ref, mine_a_ref, mine_b_ref, cur, dxs, dys):
    finish(l_ref, prev_ref, next_ref, in_ref, cur)
    rates(cur[...], dx_ref, dy_ref, dxs, dys)
    move(lambda at, n: cur[pl.ds(at, n), :], tend_ref, mrow_ref, out_ref, dxs, dys, m_ref, mine_a_ref, mine_b_ref)


def place_kernel(arrived_hbm, out_hbm, arrived_ref, cur, sems):
    pltpu.sync_copy(arrived_hbm, arrived_ref)
    rows = arrived_ref[...].reshape(COLS, WIDE)
    place_col = rows[:, ROWS:ROWS + 1]
    pick = jnp.where(iota((COLS, COLS), 1).astype(F32) == place_col, 1.0, 0.0).astype(BF16)
    hi, lo = split2(jnp.transpose(rows)[0:ROWS, :])

    def body(done):
        for at in CHUNKS:
            cur[at, :] = dot(hi[at], pick) + dot(lo[at], pick)
            done(at)

    storing(body, cur, out_hbm, sems)


def call(kernel, out, specs, scratch=(), semaphores=0, hbm_out=0):
    shapes = tuple((pltpu.HBM if k < hbm_out else pltpu.VMEM)(s, t) for k, (s, t) in enumerate(out))
    work = [pltpu.VMEM(s, t) for s, t in scratch]
    if semaphores:
        work.append(pltpu.SemaphoreType.DMA((semaphores,)))
    return pl.pallas_call(
        kernel, out_shape=shapes, in_specs=specs, out_specs=(HB,) * hbm_out + (VM,) * (len(out) - hbm_out),
        scratch_shapes=work, compiler_params=PARAMS)


def in_hbm(*arrays):
    return tuple(pltpu.with_memory_space_constraint(a, pltpu.HBM) for a in arrays)


def swapped(array, first):
    length = lax.axis_size(AXES)
    low = range(0 if first else 1, length, 2)
    pairs = [(i, (i + 1) % length) for i in low]
    return lax.ppermute(array, AXES, pairs + [(j, i) for i, j in pairs])


def step(state, metric, neighbours, cost_class, batch_slot, level_mix, field_coupling_matrix):
    me = lax.axis_index(AXES).astype(jnp.int32).reshape(1)
    base = me * MEMBERS
    state2 = state.reshape(ROWS, COLS)
    dx, dy = (jnp.asarray(a) for a in derivative_blocks())
    send, tend, m, mine_a, mine_b, out_rows, in_rows, mrow = physics_call(
        state2, cost_class, batch_slot, level_mix, field_coupling_matrix, me, metric, neighbours, dx, dy)
    (whole,) = call(whole_kernel, [((COLS, COLS), BF16)], [SM, VM])(base, neighbours)
    arrived = lax.all_to_all(send, AXES, split_axis=0, concat_axis=0, tiled=True)
    for substep in range(SUBSTEPS):
        theirs_b = swapped(mine_b, False)
        theirs_a = swapped(mine_a, True)
        (total,) = call(sum_kernel, [MOVED], [VM, VM])(m, whole)
        if substep < SUBSTEPS - 1:
            m, mine_a, mine_b = call(next_kernel, [MOVED, HALO, HALO], [VM] * 9, [GRID] * 3)(
                total, theirs_a, theirs_b, in_rows, tend, mrow, dx, dy, out_rows)
    (physics_state,) = call(place_kernel, [GRID], [HB], [((COLS // 4, 4, WIDE), F32), GRID], len(CHUNKS), 1)(
        *in_hbm(arrived))
    (state_out,) = call(finish_kernel, [GRID], [VM] * 4, [GRID], len(CHUNKS), 1)(
        total, theirs_a, theirs_b, in_rows)
    return state_out.reshape(state.shape), physics_state.reshape(state.shape)


def solution(mesh):
    split = P(None, AXES)
    whole = P(None, None, AXES)
    return jax.shard_map(
        step, mesh=mesh, in_specs=(whole, split, split, split, P(), P(), P()),
        out_specs=(whole, whole), check_vma=False)
```

```python
import jax
import jax.numpy as jnp
import numpy as np
from jax import lax
from jax.experimental import pallas as pl
from jax.experimental.pallas import tpu as pltpu
from jax.sharding import PartitionSpec as P


AXES = ("elem", "face")
F32 = jnp.float32
BF16 = jnp.bfloat16
HIGHEST = lax.Precision.HIGHEST
FIELDS, LEVELS, SUBSTEPS = 10, 72, 3
ROWS, COLS, MEMBERS, WIDE = 720, 512, 32, 768
TALL = ROWS + 8
PHYSICS_RATE, TIME_STEP = 0.1, 0.02
VM = pl.BlockSpec(memory_space=pltpu.VMEM)
HB = pl.BlockSpec(memory_space=pltpu.HBM)
SM = pl.BlockSpec(memory_space=pltpu.SMEM)
PARAMS = pltpu.CompilerParams(vmem_limit_bytes=30 << 20)


def gll_matrix():
    nodes = np.array([-1.0, -1.0 / np.sqrt(5.0), 1.0 / np.sqrt(5.0), 1.0])
    derivative = np.zeros((4, 4))
    for i in range(4):
        for j in range(4):
            others = [k for k in range(4) if k != j]
            if i == j:
                derivative[i, j] = sum(1.0 / (nodes[j] - nodes[k]) for k in others)
            else:
                top = np.prod([nodes[i] - nodes[k] for k in others if k != i])
                derivative[i, j] = top / np.prod([nodes[j] - nodes[k] for k in others])
    return derivative


def derivative_blocks():
    d = gll_matrix()
    across = np.kron(np.eye(4), d).astype(np.float32).T
    upward = np.kron(d, np.eye(4)).astype(np.float32).T
    return np.kron(np.eye(16), across).astype(np.float32), np.kron(np.eye(16), upward).astype(np.float32)


SIZES = (160, 288, 416, COLS)


def split2(v):
    hi = v.astype(BF16)
    return hi, (v - hi.astype(F32)).astype(BF16)


def dot(a, b):
    return jnp.dot(a, b, preferred_element_type=F32)


def dot_nt(a, b):
    return lax.dot_general(a, b, (((1,), (1,)), ((), ())), preferred_element_type=F32)


def iota(shape, dim):
    return lax.broadcasted_iota(jnp.int32, shape, dim)


def expand_points(table):
    spread = jnp.where(iota((32, COLS), 1) // 16 == iota((32, COLS), 0), 1.0, 0.0)
    wide = jnp.dot(table, spread, precision=HIGHEST, preferred_element_type=F32)
    wide = jnp.where(iota((16, COLS), 1) % 16 == iota((16, COLS), 0), wide, 0.0)
    return jnp.sum(wide, axis=0, keepdims=True)


def as_column(row):
    return jnp.transpose(jnp.broadcast_to(row, (8, COLS)))[:, 0:1]


def rank_row(key_row):
    key_col = as_column(key_row)
    return jnp.sum(jnp.where(key_col < key_row, 1.0, 0.0), axis=0, keepdims=True)


def physics_kernel(me_ref, fcm_hbm, state_hbm, class_hbm, slots_hbm, mix_hbm, metric_hbm, nb_hbm, dx_hbm, dy_hbm,
                   send_hbm, tend_ref, m_ref, mine_a_ref, mine_b_ref, out_ref, in_ref, mrow_ref,
                   k32, kk, state_ref, class_ref, slot_ref, mix_ref, x0, yy, tt, rr, qa, qb, send_ref,
                   metric_ref, nb_ref, dx_ref, dy_ref, dxs, dys, fcm_ref, sems):
    me = me_ref[0]
    load_slots = pltpu.make_async_copy(
        slots_hbm.at[:, pl.ds(pl.multiple_of(me // 4 * 128, 128), 128)], slot_ref, sems.at[0])
    load_state = pltpu.make_async_copy(state_hbm, state_ref, sems.at[1])
    load_class = pltpu.make_async_copy(class_hbm, class_ref, sems.at[2])
    load_mix = pltpu.make_async_copy(mix_hbm, mix_ref, sems.at[3])
    load_fcm = pltpu.make_async_copy(fcm_hbm, fcm_ref, sems.at[4])
    load_metric = pltpu.make_async_copy(metric_hbm, metric_ref, sems.at[5])
    load_nb = pltpu.make_async_copy(nb_hbm, nb_ref, sems.at[6])
    load_dx = pltpu.make_async_copy(dx_hbm, dx_ref, sems.at[7])
    load_dy = pltpu.make_async_copy(dy_hbm, dy_ref, sems.at[8])
    load_fcm.start()
    load_mix.start()
    load_slots.start()
    load_class.start()
    load_state.start()
    load_nb.start()
    load_metric.start()
    load_dx.start()
    load_dy.start()
    for load in (load_fcm, load_mix, load_slots, load_class, load_nb, load_metric, load_dx, load_dy, load_state):
        load.wait()
    tables(me * MEMBERS, nb_ref, metric_ref, out_ref, in_ref, mrow_ref)
    rep = jnp.where(
        (iota((LEVELS, WIDE), 1) % LEVELS == iota((LEVELS, WIDE), 0)) & (iota((LEVELS, WIDE), 1) < ROWS), 1.0, 0.0
    ).astype(BF16)
    lane = iota((1, WIDE), 1)
    for f in range(FIELDS):
        crow = jnp.zeros((1, WIDE), F32)
        for g in range(FIELDS):
            crow = jnp.where((lane >= LEVELS * g) & (lane < LEVELS * g + LEVELS), PHYSICS_RATE * fcm_ref[g, f], crow)
        mh, ml = split2(jnp.transpose(mix_ref[f]))
        k32[LEVELS * f:LEVELS * f + LEVELS, :] = (dot(mh, rep) + dot(ml, rep)) * crow
    k32[ROWS:WIDE, :] = jnp.zeros((WIDE - ROWS, WIDE), F32)
    hi, lo = split2(k32[...])
    kk[0:WIDE, :] = hi
    kk[WIDE:, :] = lo
    part = me % 4
    own = slot_ref[:, 0:MEMBERS]
    for j in range(1, 4):
        own = jnp.where(part == j, slot_ref[:, MEMBERS * j:MEMBERS * j + MEMBERS], own)
    cls = expand_points(class_ref[...].astype(F32))
    slot = expand_points(own.astype(F32))
    col = iota((1, COLS), 1).astype(F32)
    crank = rank_row((4.0 - cls) * COLS + col)
    srank = rank_row(slot)
    place = slot - jnp.floor(slot * (1.0 / COLS)) * COLS
    perm = jnp.where(iota((COLS, COLS), 0).astype(F32) == crank, 1.0, 0.0).astype(BF16)
    extra = jnp.where(iota((128, COLS), 0) == 0, place, 0.0)
    eh, el = split2(extra)
    x0[:, ROWS:WIDE] = (dot_nt(perm, eh) + dot_nt(perm, el))[:, 0:WIDE - ROWS]
    rh, rl = split2(jnp.broadcast_to(srank, (16, COLS)))
    srank_sorted = (dot_nt(rh, perm) + dot_nt(rl, perm))[0:1, :]
    n1 = jnp.sum(jnp.where(cls > 1.5, 1, 0))
    n2 = jnp.sum(jnp.where(cls > 2.5, 1, 0))
    n3 = jnp.sum(jnp.where(cls > 3.5, 1, 0))
    sh, sl = split2(state_ref[...])
    x0[:, 0:ROWS] = dot_nt(perm, sh) + dot_nt(perm, sl)
    rates(state_ref[...], dx_ref, dy_ref, dxs, dys)
    xh, xl = split2(x0[...])
    xhh = jnp.concatenate([xh, xh], axis=1)
    y = (dot(xl, kk[0:WIDE, :]) + dot(xhh, kk[...])) * (1.0 / PHYSICS_RATE)
    yy[...] = y
    t = jnp.tanh(y)
    tt[...] = t
    q = t.astype(BF16)
    rr[...] = t - q.astype(F32)
    qa[...] = q

    def step(rows, live, old, new, low):
        deep = 2 * WIDE if low else WIDE
        acc = dot(old[0:rows, 0:deep], kk[0:deep, :])
        for b in range(0, rows, 32):
            rb = slice(b, b + 32)
            y = yy[rb, :] + acc[rb]
            yy[rb, :] = y
            t = jnp.tanh(y)
            if b + 32 > max((0,) + tuple(n for n in SIZES if n < rows)):
                tt[rb, :] += jnp.where(iota((32, WIDE), 0) + b < live, t, 0.0)
            else:
                tt[rb, :] += t
            s = t + rr[rb, :]
            q = s.astype(BF16)
            rr[rb, :] = s - q.astype(F32)
            new[rb, 0:WIDE] = q
            if not low:
                new[rb, WIDE:] = (old[rb, 0:WIDE].astype(F32) + q.astype(F32)).astype(BF16)

    def sweep(k, old, new, low):
        live = jnp.where(k < 4, COLS, jnp.where(k < 8, n1, jnp.where(k < 12, n2, jnp.where(k < 16, n3, 0))))
        for below, rows in zip((0,) + SIZES, SIZES):
            @pl.when((live > below) & (live <= rows))
            def _():
                step(rows, live, old, new, low)

    def two_sweeps(j, _):
        sweep(2 * j + 1, qa, qb, False)
        sweep(2 * j + 2, qb, qa, True)
        return 0

    lax.fori_loop(0, 8, two_sweeps, 0)
    q_send = jnp.where(iota((COLS, COLS), 0).astype(F32) == srank_sorted, 1.0, 0.0).astype(BF16)
    fh, fl = split2(x0[...] + PHYSICS_RATE * tt[...])
    out = dot(jnp.concatenate([q_send, q_send], axis=1), jnp.concatenate([fh, fl], axis=0))
    send_ref[...] = out.reshape(COLS // 4, 4, WIDE)
    store_send = pltpu.make_async_copy(send_ref, send_hbm, sems.at[9])
    store_send.start()
    th, tl = split2(jnp.transpose(tt[...])[0:ROWS, :] * (PHYSICS_RATE / SUBSTEPS))
    tend_ref[...] = dot(jnp.concatenate([th, tl], axis=1), jnp.concatenate([perm, perm], axis=0))
    move(lambda at, n: state_ref[pl.ds(at, n), :], tend_ref, mrow_ref, out_ref, dxs, dys, m_ref, mine_a_ref, mine_b_ref)
    store_send.wait()


HALO = ((MEMBERS, WIDE), F32)
MOVED = ((TALL, COLS), F32)
GRID = ((ROWS, COLS), F32)


def physics_call(state2, cost_class, batch_slot, level_mix, fcm, me, metric, neighbours, dx, dy):
    work = [((WIDE, WIDE), F32), ((2 * WIDE, WIDE), BF16), GRID, ((16, MEMBERS), jnp.int32),
            ((16, 128), jnp.int32), ((FIELDS, LEVELS, LEVELS), F32)]
    work += [((COLS, WIDE), F32)] * 4 + [((COLS, WIDE), BF16), ((COLS, 2 * WIDE), BF16), ((COLS // 4, 4, WIDE), F32)]
    work += [((16, MEMBERS), F32), ((4, MEMBERS), jnp.int32), ((256, 256), F32), ((256, 256), F32), GRID, GRID]
    out = [((COLS // 4, 4, WIDE), F32), GRID, MOVED, HALO, HALO, ((2 * MEMBERS, COLS), BF16),
           ((2 * MEMBERS, COLS), BF16), ((8, COLS), F32)]
    shapes = tuple((pltpu.HBM if k < 1 else pltpu.VMEM)(s, t) for k, (s, t) in enumerate(out))
    return pl.pallas_call(
        physics_kernel, out_shape=shapes, in_specs=[SM] + [HB] * 9, out_specs=(HB,) + (VM,) * 7,
        scratch_shapes=[pltpu.VMEM(s, t) for s, t in work]
        + [pltpu.SMEM((FIELDS, FIELDS), F32), pltpu.SemaphoreType.DMA((10,))],
        compiler_params=PARAMS, name="physics",
    )(me, *in_hbm(fcm, state2, cost_class, batch_slot, level_mix, metric, neighbours, dx, dy))


def element_tables(neighbours_ref, base):
    local = neighbours_ref[...] - base
    outside = (local < 0) | (local >= MEMBERS)
    wide = jnp.concatenate([local.astype(F32), jnp.where(outside, 1.0, 0.0)], axis=0)
    spread = jnp.where(iota((MEMBERS, COLS), 1) // 16 == iota((MEMBERS, COLS), 0), 1.0, 0.0)
    by_column = jnp.dot(wide, spread, precision=HIGHEST, preferred_element_type=F32)
    return wide, by_column, spread


def east_west(by_column):
    col = iota((1, COLS), 1)
    ix, line = col % 4, (col % 16) // 4 * 4
    source = jnp.where(ix == 3, 16.0 * by_column[0:1] + line.astype(F32),
                       jnp.where(ix == 0, 16.0 * by_column[1:2] + (line + 3).astype(F32), -1.0))
    row = iota((COLS, COLS), 0)
    hit = (row.astype(F32) == source) | (row == iota((COLS, COLS), 1))
    return jnp.where(hit, 1.0, 0.0).astype(BF16)


def north_south(by_column):
    col = iota((1, COLS), 1)
    ix, iy = (col % 4).astype(F32), (col % 16) // 4
    north = jnp.where(by_column[6:7] > 0.5, -1.0, 16.0 * by_column[2:3] + ix)
    south = jnp.where(by_column[7:8] > 0.5, -1.0, 16.0 * by_column[3:4] + 12.0 + ix)
    source = jnp.where(iy == 3, north, jnp.where(iy == 0, south, -1.0))
    row = iota((COLS, COLS), 0)
    hit = (row.astype(F32) == source) | (row == iota((COLS, COLS), 1))
    return jnp.where(hit, 1.0, 0.0).astype(BF16)


def rank_among(key, member, spread):
    key8 = jnp.broadcast_to(jnp.where(member > 0.5, key, 1e9), (8, MEMBERS))
    key_col = jnp.transpose(key8)[:, 0:1]
    rank = jnp.sum(jnp.where(key_col < key, 1.0, 0.0), axis=0, keepdims=True)
    return jnp.dot(jnp.broadcast_to(rank, (8, MEMBERS)), spread, precision=HIGHEST,
                   preferred_element_type=F32)[0:1]


def halo_targets(wide, by_column, spread):
    col = iota((1, COLS), 1)
    ix, iy = (col % 4).astype(F32), (col % 16) // 4
    own = iota((1, MEMBERS), 1).astype(F32)
    up, down = by_column[6:7] > 0.5, by_column[7:8] > 0.5
    to_north = jnp.where((iy == 3) & up, 8.0 * ix + rank_among(own, wide[6:7], spread), -1.0)
    to_south = jnp.where((iy == 0) & down, 8.0 * ix + rank_among(own, wide[7:8], spread), -1.0)
    from_south = jnp.where((iy == 0) & down, 8.0 * ix + rank_among(wide[3:4], wide[7:8], spread), -1.0)
    from_north = jnp.where((iy == 3) & up, 8.0 * ix + rank_among(wide[2:3], wide[6:7], spread), -1.0)
    return to_north, to_south, from_south, from_north


def two_selections(first, second):
    row = iota((2 * MEMBERS, COLS), 0).astype(F32)
    hit = (row == first) | ((row - MEMBERS == second) & (second > -0.5))
    return jnp.where(hit, 1.0, 0.0).astype(BF16)


def whole_kernel(base_ref, neighbours_ref, whole_ref):
    base = base_ref[0]
    _, by_column, _ = element_tables(neighbours_ref, base)
    whole_ref[...] = dot(east_west(by_column), north_south(by_column)).astype(BF16)


def tables(base, neighbours_ref, metric_ref, out_ref, in_ref, mrow_ref):
    wide, by_column, spread = element_tables(neighbours_ref, base)
    to_north, to_south, from_south, from_north = halo_targets(wide, by_column, spread)
    odd = base // MEMBERS % 2 == 1
    sent = two_selections(jnp.where(odd, to_south, to_north), jnp.where(odd, to_north, to_south))
    out_ref[...] = dot_nt(sent, east_west(by_column)).astype(BF16)
    in_ref[...] = two_selections(jnp.where(odd, from_south, from_north), jnp.where(odd, from_north, from_south))
    mrow_ref[...] = jnp.broadcast_to(expand_points(metric_ref[...]), (8, COLS))


def rates(value, dx_ref, dy_ref, dxs, dys):
    vh, vl = split2(value)
    for half in (0, 256):
        at = slice(half, half + 256)
        parts = jnp.concatenate([vh[:, at], vl[:, at], vh[:, at]], axis=1)
        for d_ref, acc in ((dx_ref, dxs), (dy_ref, dys)):
            dh, dl = split2(d_ref[...])
            acc[:, at] = dot(parts, jnp.concatenate([dh, dh, dl], axis=0))


def move(read, tend_ref, mrow_ref, out_ref, dxs, dys, m_ref, mine_a_ref, mine_b_ref):
    metric = mrow_ref[0:1, :]
    u, v = read(0, LEVELS), read(LEVELS, LEVELS)
    for f in range(FIELDS):
        at = pl.ds(LEVELS * f, LEVELS)
        rate = u * dxs[at, :] + v * dys[at, :]
        m_ref[at, :] = metric * ((read(LEVELS * f, LEVELS) - TIME_STEP * rate) + tend_ref[at, :])
    m_ref[ROWS:TALL, :] = mrow_ref[...]
    mh, ml = split2(m_ref[...])
    halo = dot_nt(out_ref[...], mh) + dot_nt(out_ref[...], ml)
    mine_a_ref[:, 0:TALL] = halo[0:MEMBERS]
    mine_b_ref[:, 0:TALL] = halo[MEMBERS:]
    mine_a_ref[:, TALL:WIDE] = jnp.zeros((MEMBERS, WIDE - TALL), F32)
    mine_b_ref[:, TALL:WIDE] = jnp.zeros((MEMBERS, WIDE - TALL), F32)


def sum_kernel(m_ref, whole_ref, l_ref):
    mh, ml = split2(m_ref[...])
    l_ref[...] = dot(mh, whole_ref[...]) + dot(ml, whole_ref[...])


def finish(l_ref, prev_ref, next_ref, in_ref, c_ref, done=lambda at: None):
    halo = jnp.concatenate([prev_ref[...], next_ref[...]], axis=0)
    hh, hl = split2(jnp.transpose(halo)[0:TALL, :])
    mass = l_ref[ROWS:TALL, :] + dot(hh[ROWS:TALL], in_ref[...]) + dot(hl[ROWS:TALL], in_ref[...])
    inverse = 1.0 / mass[0:1, :]
    for at in CHUNKS:
        c_ref[at, :] = (l_ref[at, :] + dot(hh[at], in_ref[...]) + dot(hl[at], in_ref[...])) * inverse
        done(at)


CHUNKS = tuple(slice(a, a + 144) for a in range(0, ROWS, 144))


def storing(body, source, target, sems):
    copies = []

    def done(at):
        copies.append(pltpu.make_async_copy(source.at[at], target.at[at], sems.at[len(copies)]))
        copies[-1].start()

    body(done)
    for copy in copies:
        copy.wait()


def finish_kernel(l_ref, prev_ref, next_ref, in_ref, out_hbm, cur, sems):
    storing(lambda done: finish(l_ref, prev_ref, next_ref, in_ref, cur, done), cur, out_hbm, sems)


def next_kernel(l_ref, prev_ref, next_ref, in_ref, tend_ref, mrow_ref, dx_ref, dy_ref, out_ref,
                m_ref, mine_a_ref, mine_b_ref, cur, dxs, dys):
    finish(l_ref, prev_ref, next_ref, in_ref, cur)
    rates(cur[...], dx_ref, dy_ref, dxs, dys)
    move(lambda at, n: cur[pl.ds(at, n), :], tend_ref, mrow_ref, out_ref, dxs, dys, m_ref, mine_a_ref, mine_b_ref)


def place_kernel(arrived_hbm, out_hbm, arrived_ref, cur, sems):
    pltpu.sync_copy(arrived_hbm, arrived_ref)
    rows = arrived_ref[...].reshape(COLS, WIDE)
    place_col = rows[:, ROWS:ROWS + 1]
    pick = jnp.where(iota((COLS, COLS), 1).astype(F32) == place_col, 1.0, 0.0).astype(BF16)
    hi, lo = split2(jnp.transpose(rows)[0:ROWS, :])

    def body(done):
        for at in CHUNKS:
            cur[at, :] = dot(hi[at], pick) + dot(lo[at], pick)
            done(at)

    storing(body, cur, out_hbm, sems)


def call(kernel, out, specs, scratch=(), semaphores=0, hbm_out=0):
    shapes = tuple((pltpu.HBM if k < hbm_out else pltpu.VMEM)(s, t) for k, (s, t) in enumerate(out))
    work = [pltpu.VMEM(s, t) for s, t in scratch]
    if semaphores:
        work.append(pltpu.SemaphoreType.DMA((semaphores,)))
    return pl.pallas_call(
        kernel, out_shape=shapes, in_specs=specs, out_specs=(HB,) * hbm_out + (VM,) * (len(out) - hbm_out),
        scratch_shapes=work, compiler_params=PARAMS)


def in_hbm(*arrays):
    return tuple(pltpu.with_memory_space_constraint(a, pltpu.HBM) for a in arrays)


def swapped(array, first):
    length = lax.axis_size(AXES)
    low = range(0 if first else 1, length, 2)
    pairs = [(i, (i + 1) % length) for i in low]
    return lax.ppermute(array, AXES, pairs + [(j, i) for i, j in pairs])


def step(state, metric, neighbours, cost_class, batch_slot, level_mix, field_coupling_matrix):
    me = lax.axis_index(AXES).astype(jnp.int32).reshape(1)
    base = me * MEMBERS
    state2 = state.reshape(ROWS, COLS)
    dx, dy = (jnp.asarray(a) for a in derivative_blocks())
    send, tend, m, mine_a, mine_b, out_rows, in_rows, mrow = physics_call(
        state2, cost_class, batch_slot, level_mix, field_coupling_matrix, me, metric, neighbours, dx, dy)
    (whole,) = call(whole_kernel, [((COLS, COLS), BF16)], [SM, VM])(base, neighbours)
    arrived = lax.all_to_all(send, AXES, split_axis=0, concat_axis=0, tiled=True)
    for substep in range(SUBSTEPS):
        theirs_b = swapped(mine_b, False)
        theirs_a = swapped(mine_a, True)
        (total,) = call(sum_kernel, [MOVED], [VM, VM])(m, whole)
        if substep < SUBSTEPS - 1:
            m, mine_a, mine_b = call(next_kernel, [MOVED, HALO, HALO], [VM] * 9, [GRID] * 3)(
                total, theirs_a, theirs_b, in_rows, tend, mrow, dx, dy, out_rows)
    (physics_state,) = call(place_kernel, [GRID], [HB], [((COLS // 4, 4, WIDE), F32), GRID], len(CHUNKS), 1)(
        *in_hbm(arrived))
    (state_out,) = call(finish_kernel, [GRID], [VM] * 4, [GRID], len(CHUNKS), 1)(
        total, theirs_a, theirs_b, in_rows)
    return state_out.reshape(state.shape), physics_state.reshape(state.shape)


def solution(mesh):
    split = P(None, AXES)
    whole = P(None, None, AXES)
    return jax.shard_map(
        step, mesh=mesh, in_specs=(whole, split, split, split, P(), P(), P()),
        out_specs=(whole, whole), check_vma=False)
```
